32 devices in a mesh: row: 4 (over x, core), col: 8 (over z, y).
Axes of the slice: x: 2, y: 2, z: 4, core: 2. Of those that a mesh axis runs over, the one named last changes fastest.
Arguments:
- matrix: float32 [8, 512, 4, 1024], P(None, 'row', None, 'col'), as said below
Outputs:
- factored: float32 [8, 512, 4, 1024], P(None, 'row', None, 'col')
Inputs may be any that keep to these rules, and one draw needn't show every extreme that they name: `matrix`: Symmetric; an exponential covariance kernel exp(-distance / reach) between sites in three dimensions, plus a diagonal noise variance of 0.5 or more at each site, so every Schur complement taken during the factorization is positive definite.
All inputs are finite; a program needn't handle non-finite values.
Results may differ from the reference program's by a relative error of at most 0.00011.
Values sent between devices are 32-bit elements; how exact they have to be, the bound alone decides.
No kernel may reach another device: no remote copies, remote signals or barrier semaphores. Data moves between devices by JAX's collectives and lax.ppermute only.
A program may use at most 128 MiB of HBM per device.

```python
import math
import jax
import jax.numpy as jnp
from jax import lax

NB = 128
CB = 4
STEPS = 8
RB = 8
ORDER = 4096


def draw_matrix(key, part):
    key_points, key_self = jax.random.split(key)
    reach = 0.12
    upper = 2.0
    points = jax.random.uniform(key_points, (ORDER, 3), jnp.float32)
    self_term = jnp.exp(jax.random.uniform(key_self, (ORDER,), jnp.float32, math.log(0.5), math.log(upper)))
    squared = jnp.zeros((ORDER, ORDER), jnp.float32)
    for axis_num in range(3):
        spread = points[:, axis_num][:, None] - points[:, axis_num][None, :]
        squared = squared + spread * spread
    kernel = jnp.exp(-jnp.sqrt(squared) / reach)
    row_index = lax.broadcasted_iota(jnp.int32, (ORDER, ORDER), 0)
    col_index = lax.broadcasted_iota(jnp.int32, (ORDER, ORDER), 1)
    filled = kernel + jnp.where(row_index == col_index, self_term[:, None], 0.0)
    return filled.reshape(RB, ORDER // RB, CB, ORDER // CB)


def setup_inputs(seed: int = 0) -> dict:
    streams_of = jax.random.split(jax.random.key(seed), 2)
    return {
        "matrix": draw_matrix(jax.random.fold_in(streams_of[1], 71), 0),
    }


def reference(matrix):
    entire = matrix.reshape(ORDER, ORDER)
    identity = jnp.eye(NB, dtype=jnp.float32)
    for panel_step in range(STEPS):
        begin_at = panel_step * NB
        end_at = begin_at + NB
        factor = jnp.linalg.cholesky(entire[begin_at:end_at, begin_at:end_at])
        inverse = jax.scipy.linalg.solve_triangular(factor, identity, lower=True)
        panel_rows = jnp.dot(entire[end_at:, begin_at:end_at].astype(jnp.float32), inverse.T.astype(jnp.float32), precision=lax.Precision.HIGHEST, preferred_element_type=jnp.float32)
        trailing = entire[end_at:, end_at:] - jnp.dot(panel_rows.astype(jnp.float32), panel_rows.T.astype(jnp.float32), precision=lax.Precision.HIGHEST, preferred_element_type=jnp.float32)
        entire = entire.at[end_at:, end_at:].set(trailing)
        entire = entire.at[begin_at:end_at, begin_at:end_at].set(factor)
        entire = entire.at[end_at:, begin_at:end_at].set(panel_rows)
        entire = entire.at[begin_at:end_at, end_at:].set(jnp.zeros((NB, ORDER - end_at), jnp.float32))
    return entire.reshape(matrix.shape)
```

```python
import functools

import jax
import jax.numpy as jnp
from jax import lax
from jax.experimental import pallas as pl
from jax.experimental.pallas import tpu as pltpu
from jax.sharding import PartitionSpec as P

STEPS = 8
PANEL = 16
F32 = jnp.float32
BF16 = jnp.bfloat16


def split2(x):
    high = x.astype(BF16)
    return high, (x - high.astype(F32)).astype(BF16)


def split3(x):
    high = x.astype(BF16)
    rest = x - high.astype(F32)
    mid = rest.astype(BF16)
    return high, mid, (rest - mid.astype(F32)).astype(BF16)


def contract(left, right, dims):
    return lax.dot_general(left, right, (dims, ((), ())), preferred_element_type=F32)


def gram(rows_in, rows_wide):
    h, m, l = split3(rows_in)
    hw, mw, lw = split3(rows_wide)
    left = jnp.concatenate([h, h, m, m, h, l], 0)
    right = jnp.concatenate([hw, mw, hw, mw, lw, hw], 0)
    return contract(left, right, ((0,), (0,)))


def three(left, right, dims):
    (lh, lm), (rh, rm) = left, right
    return contract(lh, rh, dims) + (contract(lh, rm, dims) + contract(lm, rh, dims))


def factor_tile(tile, nb):
    for first in range(0, nb, PANEL):
        rows = [tile[pl.ds(first + i, 8, stride=0), :] for i in range(PANEL)]
        left = [r[:, :nb] for r in rows]
        right = [r[:, nb:] for r in rows]
        entry = {}
        for i in range(PANEL):
            for s in range(i + 1):
                lane = first + i
                entry[i, s] = jnp.broadcast_to(left[s][:, lane : lane + 1], (8, nb))
        for s in range(PANEL):
            scale = lax.rsqrt(entry[s, s])
            left[s] = left[s] * scale
            right[s] = right[s] * scale
            for i in range(s + 1, PANEL):
                entry[i, s] = entry[i, s] * scale
            for i in range(s + 1, PANEL):
                for t in range(s + 1, i + 1):
                    entry[i, t] = entry[i, t] - entry[i, s] * entry[t, s]
            for i in range(s + 1, PANEL):
                left[i] = left[i] - entry[i, s] * left[s]
                right[i] = right[i] - entry[i, s] * right[s]
        for s in range(PANEL):
            tile[first + s : first + s + 1, :nb] = left[s][:1]
            tile[first + s : first + s + 1, nb:] = right[s][:1]
        after = first + PANEL
        if after < nb:
            done = tile[first:after, :]
            tile[after:, :] = tile[after:, :] - gram(done[:, :nb], done)[after:, :]


def factor_kernel(
    place, lead, side, solved, top, tile, up_h, up_m, gk, yh, ym, mh, mm, *, nb, na, rows_dev, cols_dev, fwd
):
    my_row, my_col = place[0], place[1]
    width = STEPS * nb
    ii = lax.broadcasted_iota(jnp.int32, (nb, nb), 0)
    jj = lax.broadcasted_iota(jnp.int32, (nb, nb), 1)
    eye = jnp.where(ii == jj, 1.0, 0.0).astype(F32)
    wide_b = side.shape[1]
    ND = ((0,), (0,))
    MM = ((1,), (0,))

    @pl.loop(0, STEPS)
    def _(k):
        base = pl.multiple_of(k * nb, nb)
        for step in range(STEPS):

            @pl.when(k == step)
            def _():
                lo = step * nb
                if step == 0:
                    tile[:, :nb] = lead[:nb, :nb]
                else:
                    l = (up_h[:lo, lo : lo + nb], up_m[:lo, lo : lo + nb])
                    tile[:, :nb] = lead[lo : lo + nb, lo : lo + nb] - three(l, l, ND)

        tile[:, nb:] = eye
        factor_tile(tile, nb)
        gk[pl.ds(base, nb), :] = tile[:, nb:]
        for step in range(STEPS):

            @pl.when(k == step)
            def _():
                lo, hi = step * nb, step * nb + nb
                rest = side[lo:hi, :]
                g = split2(tile[:, nb:])
                if step:
                    l = (up_h[:lo, lo:hi], up_m[:lo, lo:hi])
                    rest = rest - three(l, (yh[:lo, :], ym[:lo, :]), ND)
                h, m = split2(three(g, split2(rest), MM))
                yh[lo:hi, :] = h
                ym[lo:hi, :] = m
                h, m = split2(jnp.where(ii <= jj, tile[:, :nb], 0.0))
                up_h[lo:hi, lo:hi] = h
                up_m[lo:hi, lo:hi] = m
                if hi < width:
                    right = lead[lo:hi, hi:]
                    if step:
                        right = right - three(l, (up_h[:lo, hi:], up_m[:lo, hi:]), ND)
                    block = three(g, split2(right), MM)
                    h, m = split2(block)
                    up_h[lo:hi, hi:] = h
                    up_m[lo:hi, hi:] = m
                mine = my_col == step
                for a in range(na):
                    for p in range(rows_dev):
                        row = a * rows_dev + p

                        @pl.when(mine & (my_row == p))
                        def _():
                            if row < step:
                                top[a] = jnp.zeros((nb, nb), F32)
                            elif row == step:
                                top[a] = jnp.where(ii >= jj, tile[:, :nb].T, 0.0)
                            else:
                                at = row * nb - hi
                                top[a] = block[:, at : at + nb].T

    @pl.when(my_col >= STEPS)
    def _():
        top[...] = jnp.zeros(top.shape, F32)

    for step in reversed(range(STEPS)):
        lo, hi = step * nb, step * nb + nb
        lead_part = jnp.where(my_col == step, eye, 0.0)
        known_h, known_m = yh[lo:hi, :], ym[lo:hi, :]
        known = known_h.astype(F32) + known_m.astype(F32)
        if fwd == 0:
            lead_part = jnp.where(my_col < STEPS, lead_part, known[:, :nb])
            known = known[:, nb:]
        rest = jnp.concatenate([lead_part, known], 1)
        if hi < width:
            rest = rest - three((up_h[lo:hi, hi:], up_m[lo:hi, hi:]), (mh[hi:, :], mm[hi:, :]), MM)
        h, m = split2(three(split2(gk[lo:hi, :]), split2(rest), ND))
        mh[lo:hi, :] = h
        mm[lo:hi, :] = m
    solved[0] = mh[...]
    solved[1] = mm[...]


def close_kernel(place, across, mine, solved, top, out, *, nb, na, block_rows, block_cols):
    my_col = place[1]
    left = split2(across[...])
    prod = three(left, (solved[0], solved[1]), ((1,), (0,)))
    is_panel = my_col < STEPS
    for a in range(block_rows):
        for b in range(block_cols):
            where = pl.ds(a * nb * block_cols + b, nb, stride=block_cols)
            if a < na:
                out[where, :] = top[a] if b == 0 else jnp.zeros((nb, nb), F32)
            else:
                part = prod[(a - na) * nb : (a - na + 1) * nb, b * nb : (b + 1) * nb]
                old = mine[where, :]
                if b == 0:
                    out[where, :] = jnp.where(is_panel, part, old - part)
                else:
                    out[where, :] = old - part


def local(matrix):
    rows_dev = lax.axis_size("row")
    cols_dev = lax.axis_size("col")
    my_row = lax.axis_index("row")
    my_col = lax.axis_index("col")
    block_rows, nb, block_cols, _ = matrix.shape
    na = STEPS // rows_dev
    fwd = STEPS // cols_dev
    width = STEPS * nb
    place = jnp.stack([my_row, my_col]).astype(jnp.int32)

    first = matrix[:na, :, 0, :]
    lead = lax.all_gather(first, ("row", "col"))
    lead = lead.reshape(rows_dev, cols_dev, na, nb, nb)[:, :STEPS]
    lead = lead.transpose(2, 0, 3, 1, 4).reshape(width, width)
    side = matrix[:na, :, fwd:, :]
    side = lax.all_gather(side, "row")
    side = side.transpose(1, 0, 2, 3, 4).reshape(width, (block_cols - fwd) * nb)
    across = lax.all_gather(matrix[na:, :, 0, :], "col")[:STEPS]
    across = across.transpose(1, 2, 0, 3).reshape((block_rows - na) * nb, width)

    wide = block_cols * nb
    vmem = pl.BlockSpec(memory_space=pltpu.VMEM)
    smem = pl.BlockSpec(memory_space=pltpu.SMEM)
    solved, top = pl.pallas_call(
        functools.partial(
            factor_kernel, nb=nb, na=na, rows_dev=rows_dev, cols_dev=cols_dev, fwd=fwd
        ),
        out_shape=[
            jax.ShapeDtypeStruct((2, width, wide), BF16),
            jax.ShapeDtypeStruct((na, nb, nb), F32),
        ],
        in_specs=[smem, vmem, vmem],
        out_specs=[vmem, vmem],
        scratch_shapes=[
            pltpu.VMEM((nb, 2 * nb), F32),
            pltpu.VMEM((width, width), BF16),
            pltpu.VMEM((width, width), BF16),
            pltpu.VMEM((width, nb), F32),
            pltpu.VMEM((width, side.shape[1]), BF16),
            pltpu.VMEM((width, side.shape[1]), BF16),
            pltpu.VMEM((width, wide), BF16),
            pltpu.VMEM((width, wide), BF16),
        ],
        compiler_params=pltpu.CompilerParams(vmem_limit_bytes=56 << 20),
        name="factor",
    )(place, lead, side)
    out = pl.pallas_call(
        functools.partial(close_kernel, nb=nb, na=na, block_rows=block_rows, block_cols=block_cols),
        out_shape=jax.ShapeDtypeStruct((block_rows * nb * block_cols, nb), F32),
        in_specs=[smem, vmem, vmem, vmem, vmem],
        out_specs=vmem,
        compiler_params=pltpu.CompilerParams(vmem_limit_bytes=56 << 20),
        name="close",
    )(place, across, matrix.reshape(-1, nb), solved, top)
    return out.reshape(matrix.shape)


def solution(mesh):
    placed = (P(None, "row", None, "col"),)
    return jax.shard_map(
        local, mesh=mesh, in_specs=placed, out_specs=P(None, "row", None, "col"), check_vma=False
    )
```

```python
import functools

import jax
import jax.numpy as jnp
from jax import lax
from jax.experimental import pallas as pl
from jax.experimental.pallas import tpu as pltpu
from jax.sharding import PartitionSpec as P

STEPS = 8
PANEL = 16
F32 = jnp.float32
BF16 = jnp.bfloat16


def split2(x):
    high = x.astype(BF16)
    return high, (x - high.astype(F32)).astype(BF16)


def split3(x):
    high = x.astype(BF16)
    rest = x - high.astype(F32)
    mid = rest.astype(BF16)
    return high, mid, (rest - mid.astype(F32)).astype(BF16)


def contract(left, right, dims):
    return lax.dot_general(left, right, (dims, ((), ())), preferred_element_type=F32)


def gram(rows_in, rows_wide):
    h, m, l = split3(rows_in)
    hw, mw, lw = split3(rows_wide)
    left = jnp.concatenate([h, h, m, m, h, l], 0)
    right = jnp.concatenate([hw, mw, hw, mw, lw, hw], 0)
    return contract(left, right, ((0,), (0,)))


def three(left, right, dims):
    (lh, lm), (rh, rm) = left, right
    return contract(lh, rh, dims) + (contract(lh, rm, dims) + contract(lm, rh, dims))


def factor_tile(tile, nb, filler):
    for turn, first in enumerate(range(0, nb, PANEL)):
        rows = [tile[pl.ds(first + i, 8, stride=0), :] for i in range(PANEL)]
        left = [r[:, :nb] for r in rows]
        right = [r[:, nb:] for r in rows]
        entry = {}
        for i in range(PANEL):
            for s in range(i + 1):
                lane = first + i
                entry[i, s] = jnp.broadcast_to(left[s][:, lane : lane + 1], (8, nb))
        for s in range(PANEL):
            scale = lax.rsqrt(entry[s, s])
            left[s] = left[s] * scale
            right[s] = right[s] * scale
            for i in range(s + 1, PANEL):
                entry[i, s] = entry[i, s] * scale
            for i in range(s + 1, PANEL):
                for t in range(s + 1, i + 1):
                    entry[i, t] = entry[i, t] - entry[i, s] * entry[t, s]
            for i in range(s + 1, PANEL):
                left[i] = left[i] - entry[i, s] * left[s]
                right[i] = right[i] - entry[i, s] * right[s]
        for s in range(PANEL):
            tile[first + s : first + s + 1, :nb] = left[s][:1]
            tile[first + s : first + s + 1, nb:] = right[s][:1]
        filler(turn)
        after = first + PANEL
        if after < nb:
            done = tile[first:after, :]
            tile[after:, :] = tile[after:, :] - gram(done[:, :nb], done)[after:, :]


def sweep_kernel(*refs, phase, last, nb, na, rows_dev, cols_dev, fwd, n_pieces, n_low):
    place = refs[0]
    pieces = refs[1 : 1 + n_pieces]
    side = refs[1 + n_pieces]
    refs = refs[2 + n_pieces :]
    if phase:
        old, old_col, old_top = refs[:3]
        refs = refs[3:]
    outs, (grid_ref, col_ref, tile, lcol, rrow) = refs[:-5], refs[-5:]
    my_row, my_col = place[0], place[1]
    lead = STEPS * nb
    c0 = phase * rows_dev * nb
    rows = c0 + rows_dev * nb
    n_side = side.shape[2]
    wide = lead + n_side * nb
    top = outs[-1]
    ii = lax.broadcasted_iota(jnp.int32, (nb, nb), 0)
    jj = lax.broadcasted_iota(jnp.int32, (nb, nb), 1)
    eye = jnp.where(ii == jj, 1.0, 0.0).astype(F32)
    MM = ((1,), (0,))

    for array, (back_hi, back_lo) in zip(
        pieces, [(h, l) for l in range(2) for h in range(rows_dev // 2)], strict=True
    ):
        row_hi = lax.rem(my_row // 2 - back_hi + rows_dev // 2, rows_dev // 2)
        row_lo = lax.rem(lax.rem(my_row, 2) + back_lo, 2)
        at = pl.multiple_of(c0 + (row_hi * 2 + row_lo) * nb, nb)
        n_high = cols_dev // n_low
        for i in range(cols_dev):
            back_l, back_h = i // n_high, i % n_high
            col_hi = lax.rem(my_col // n_low - back_h + n_high, n_high)
            col_lo = lax.rem(lax.rem(my_col, n_low) - back_l + n_low, n_low)
            col = col_hi * n_low + col_lo

            @pl.when(col < STEPS)
            def _():
                grid_ref[pl.ds(at, nb), pl.ds(pl.multiple_of(col * nb, nb), nb)] = array[i]

    for p in range(rows_dev):
        for b in range(n_side):
            grid_ref[c0 + p * nb : c0 + p * nb + nb, lead + b * nb : lead + b * nb + nb] = side[p, phase, b]
    if phase:
        grid_ref[:c0, c0:] = old[...]
        grid_ref[c0:rows, c0:] = grid_ref[c0:rows, c0:] - three(
            split2(grid_ref[c0:rows, :c0]), split2(grid_ref[:c0, c0:]), MM
        )
        col_ref[...] = old_col[...]
        top[...] = old_top[...]
    else:
        col_ref[...] = jnp.zeros(col_ref.shape, F32)
        top[...] = jnp.zeros(top.shape, F32)
    lcol[...] = jnp.zeros(lcol.shape, BF16)
    rrow[...] = jnp.zeros(rrow.shape, BF16)

    def pending(i):
        at = slice(i * nb, i * nb + nb)
        grid_ref[at, c0:] = grid_ref[at, c0:] - three((lcol[0, at, :], lcol[1, at, :]), (rrow[0], rrow[1]), MM)

    @pl.loop(phase * rows_dev, (phase + 1) * rows_dev)
    def _(k):
        base = pl.multiple_of(k * nb, nb)
        here = pl.ds(base, nb)
        inner = pl.ds(pl.multiple_of(base - c0, nb), nb)
        tile[:, :nb] = grid_ref[here, here] - three(
            (lcol[0, here, :], lcol[1, here, :]), (rrow[0, :, inner], rrow[1, :, inner]), MM
        )
        tile[:, nb:] = eye

        def filler(turn):
            for i in range(rows // nb):
                if i % (nb // PANEL) == turn:
                    pending(i)

        factor_tile(tile, nb, filler)
        g = tile[:, nb:]
        gs = split2(g)

        @pl.when(k == my_col)
        def _():
            for a in range(na):
                row = a * rows_dev + my_row

                @pl.when(row == k)
                def _():
                    top[a] = jnp.where(ii >= jj, tile[:, :nb].T, 0.0)

                @pl.when(row > k)
                def _():
                    block = grid_ref[here, pl.ds(pl.multiple_of(row * nb, nb), nb)]
                    top[a] = three(gs, split2(block), MM).T

            at = lax.broadcasted_iota(jnp.int32, (rows, nb), 0)
            found = three(split2(grid_ref[:rows, here]), gs, ((1,), (1,)))
            col_ref[:rows, :] = jnp.where(at < base, -found, 0.0)
            col_ref[here, :] = g.T

        r = three(split2(gram(g, g)), split2(grid_ref[here, c0:]), MM)
        at = lax.broadcasted_iota(jnp.int32, (rows, nb), 0)
        column = jnp.where((at >= base) & (at < base + nb), 0.0, grid_ref[:rows, here])
        lcol[0], lcol[1] = split2(column)
        rrow[0], rrow[1] = split2(r)
        grid_ref[here, c0:] = r

    for i in range(rows // nb):
        pending(i)
    if last:
        solved = outs[0]
        first = col_ref[...]
        if not fwd:
            first = jnp.where(my_col < STEPS, first, grid_ref[:, lead : lead + nb])
        solved[0, :, :nb], solved[1, :, :nb] = split2(first)
        solved[0, :, nb:], solved[1, :, nb:] = split2(grid_ref[:, lead + (nb if not fwd else 0) :])
    else:
        outs[0][...] = grid_ref[:rows, rows:]
        outs[1][...] = col_ref[...]


def close_kernel(place, across, mine, solved, top, out, left_h, left_m, *, nb, na, block_rows, block_cols):
    my_col = place[1]
    for k in range(STEPS):
        at = slice(k * nb, k * nb + nb)
        left_h[:, at], left_m[:, at] = split2(across[k])
    prod = three((left_h[...], left_m[...]), (solved[0], solved[1]), ((1,), (0,)))
    is_panel = my_col < STEPS
    for a in range(block_rows):
        for b in range(block_cols):
            where = pl.ds(a * nb * block_cols + b, nb, stride=block_cols)
            if a < na:
                out[where, :] = top[a] if b == 0 else jnp.zeros((nb, nb), F32)
            else:
                part = prod[(a - na) * nb : (a - na + 1) * nb, b * nb : (b + 1) * nb]
                old = mine[where, :]
                if b == 0:
                    out[where, :] = jnp.where(is_panel, part, old - part)
                else:
                    out[where, :] = old - part


def local(matrix):
    rows_dev = lax.axis_size("row")
    cols_dev = lax.axis_size("col")
    my_row = lax.axis_index("row")
    my_col = lax.axis_index("col")
    block_rows, nb, block_cols, _ = matrix.shape
    na = STEPS // rows_dev
    fwd = STEPS // cols_dev
    lead = STEPS * nb
    wide = block_cols * nb
    n_side = block_cols - fwd
    n_low = 2
    n_high = cols_dev // n_low
    place = jnp.stack([my_row, my_col]).astype(jnp.int32)

    def step_to(x, axis, size, low, back_high, back_low):
        pairs = []
        for i in range(size):
            high, rest = divmod(i, low)
            pairs.append((i, (high + back_high) % (size // low) * low + (rest + back_low) % low))
        return lax.ppermute(x, axis, pairs)

    side = matrix[:na, :, fwd:, :].transpose(0, 2, 1, 3)
    side = lax.all_gather(side, "row")
    across = lax.all_gather(matrix[na:, :, 0, :], "col")
    across = across.reshape(cols_dev, (block_rows - na) * nb, nb)

    phases = []
    for a in range(na):
        block = matrix[a, :, 0, :]
        line = jnp.stack([block] + [step_to(block, "col", cols_dev, n_low, h, 0) for h in range(1, n_high)])
        strip = jnp.concatenate([line, step_to(line, "col", cols_dev, n_low, 0, 1)])
        near = [strip] + [step_to(strip, "row", rows_dev, 2, h, 0) for h in range(1, rows_dev // 2)]
        phases.append(near + [step_to(s, "row", rows_dev, 2, 0, 1) for s in near])

    vmem = pl.BlockSpec(memory_space=pltpu.VMEM)
    smem = pl.BlockSpec(memory_space=pltpu.SMEM)
    params = pltpu.CompilerParams(vmem_limit_bytes=56 << 20)
    carried = []
    for phase, pieces in enumerate(phases):
        last = phase == na - 1
        c0 = phase * rows_dev * nb
        rows = c0 + rows_dev * nb
        width = lead + n_side * nb
        out_shape = [jax.ShapeDtypeStruct((na, nb, nb), F32)]
        if last:
            out_shape = [jax.ShapeDtypeStruct((2, lead, wide), BF16)] + out_shape
        else:
            out_shape = [
                jax.ShapeDtypeStruct((rows, width - rows), F32),
                jax.ShapeDtypeStruct((lead, nb), F32),
            ] + out_shape
        carried = pl.pallas_call(
            functools.partial(
                sweep_kernel,
                phase=phase,
                last=last,
                nb=nb,
                na=na,
                rows_dev=rows_dev,
                cols_dev=cols_dev,
                fwd=fwd,
                n_pieces=len(pieces),
                n_low=n_low,
            ),
            out_shape=out_shape,
            in_specs=[smem] + [vmem] * (len(pieces) + 1 + len(carried)),
            out_specs=[vmem] * len(out_shape),
            scratch_shapes=[
                pltpu.VMEM((lead, width), F32),
                pltpu.VMEM((lead, nb), F32),
                pltpu.VMEM((nb, 2 * nb), F32),
                pltpu.VMEM((2, rows, nb), BF16),
                pltpu.VMEM((2, nb, width - c0), BF16),
            ],
            compiler_params=params,
            cost_estimate=pl.CostEstimate(flops=3 * 10**10, bytes_accessed=10**7, transcendentals=0),
            name="sweep%d" % phase,
        )(place, *pieces, side, *carried)
    solved, top = carried
    out = pl.pallas_call(
        functools.partial(close_kernel, nb=nb, na=na, block_rows=block_rows, block_cols=block_cols),
        out_shape=jax.ShapeDtypeStruct((block_rows * nb * block_cols, nb), F32),
        in_specs=[smem, vmem, vmem, vmem, vmem],
        out_specs=vmem,
        scratch_shapes=[pltpu.VMEM(((block_rows - na) * nb, lead), BF16)] * 2,
        compiler_params=params,
        name="close",
    )(place, across, matrix.reshape(-1, nb), solved, top)
    return out.reshape(matrix.shape)


def solution(mesh):
    placed = (P(None, "row", None, "col"),)
    return jax.shard_map(
        local, mesh=mesh, in_specs=placed, out_specs=P(None, "row", None, "col"), check_vma=False
    )
```

```python
import functools

import jax
import jax.numpy as jnp
from jax import lax
from jax.experimental import pallas as pl
from jax.experimental.pallas import tpu as pltpu
from jax.sharding import PartitionSpec as P

STEPS = 8
PANEL = 16
F32 = jnp.float32
BF16 = jnp.bfloat16


def split2(x):
    high = x.astype(BF16)
    return high, (x - high.astype(F32)).astype(BF16)


def split3(x):
    high = x.astype(BF16)
    rest = x - high.astype(F32)
    mid = rest.astype(BF16)
    return high, mid, (rest - mid.astype(F32)).astype(BF16)


def contract(left, right, dims):
    return lax.dot_general(left, right, (dims, ((), ())), preferred_element_type=F32)


def gram(rows_in, rows_wide):
    h, m, l = split3(rows_in)
    hw, mw, lw = split3(rows_wide)
    left = jnp.concatenate([h, h, m, m, h, l], 0)
    right = jnp.concatenate([hw, mw, hw, mw, lw, hw], 0)
    return contract(left, right, ((0,), (0,)))


def three(left, right, dims):
    (lh, lm), (rh, rm) = left, right
    return contract(lh, rh, dims) + (contract(lh, rm, dims) + contract(lm, rh, dims))


def factor_tile(tile, nb, filler):
    for turn, first in enumerate(range(0, nb, PANEL)):
        rows = [tile[pl.ds(first + i, 8, stride=0), :] for i in range(PANEL)]
        left = [r[:, :nb] for r in rows]
        right = [r[:, nb:] for r in rows]
        entry = {}
        for i in range(PANEL):
            for s in range(i + 1):
                lane = first + i
                entry[i, s] = jnp.broadcast_to(left[s][:, lane : lane + 1], (8, nb))
        for s in range(PANEL):
            scale = lax.rsqrt(entry[s, s])
            left[s] = left[s] * scale
            right[s] = right[s] * scale
            for i in range(s + 1, PANEL):
                entry[i, s] = entry[i, s] * scale
            for i in range(s + 1, PANEL):
                for t in range(s + 1, i + 1):
                    entry[i, t] = entry[i, t] - entry[i, s] * entry[t, s]
            for i in range(s + 1, PANEL):
                left[i] = left[i] - entry[i, s] * left[s]
                right[i] = right[i] - entry[i, s] * right[s]
        for s in range(PANEL):
            tile[first + s : first + s + 1, :nb] = left[s][:1]
            tile[first + s : first + s + 1, nb:] = right[s][:1]
        filler(turn)
        after = first + PANEL
        if after < nb:
            done = tile[first:after, :]
            tile[after:, :] = tile[after:, :] - gram(done[:, :nb], done)[after:, :]


def col_of(my_col, back_h, back_l, cols_dev, n_low):
    n_high = cols_dev // n_low
    high = lax.rem(my_col // n_low - back_h + n_high, n_high)
    return high * n_low + lax.rem(lax.rem(my_col, n_low) - back_l + n_low, n_low)


def guarded(always, condition, action):
    if always:
        action()
    else:
        pl.when(condition)(action)


def sweep_kernel(*refs, phase, last, nb, na, rows_dev, cols_dev, fwd, n_pieces, n_low):
    place = refs[0]
    pieces = refs[1 : 1 + n_pieces]
    sides = refs[1 + n_pieces : 1 + 2 * n_pieces]
    refs = refs[1 + 2 * n_pieces :]
    if phase:
        old, old_col, old_top = refs[:3]
        refs = refs[3:]
    if last:
        solved, top, solved_buf, col_ref = refs[:4]
        refs = refs[4:]
    else:
        passed, col_ref, top = refs[:3]
        refs = refs[3:]
    grid_ref, tile, held, lcol, rrow, upper, sems, out_sems = refs
    my_row, my_col = place[0], place[1]
    lead = STEPS * nb
    c0 = phase * rows_dev * nb
    rows = c0 + rows_dev * nb
    n_side = sides[0].shape[1]
    ii = lax.broadcasted_iota(jnp.int32, (nb, nb), 0)
    jj = lax.broadcasted_iota(jnp.int32, (nb, nb), 1)
    eye = jnp.where(ii == jj, 1.0, 0.0).astype(F32)
    MM = ((1,), (0,))

    lead_copies = []
    side_copies = []
    n_high = cols_dev // n_low
    for array, side, (back_hi, back_lo) in zip(
        pieces, sides, [(h, l) for l in range(2) for h in range(rows_dev // 2)], strict=True
    ):
        row_hi = lax.rem(my_row // 2 - back_hi + rows_dev // 2, rows_dev // 2)
        row_lo = lax.rem(lax.rem(my_row, 2) + back_lo, 2)
        at = pl.multiple_of(c0 + (row_hi * 2 + row_lo) * nb, nb)
        for i in range(cols_dev):
            col = col_of(my_col, i % n_high, i // n_high, cols_dev, n_low)
            copy = pltpu.make_async_copy(
                array.at[i],
                grid_ref.at[pl.ds(at, nb), pl.ds(pl.multiple_of(col * nb, nb), nb)],
                sems.at[len(lead_copies) + len(side_copies)],
            )
            lead_copies.append((col < STEPS, copy))
        for b in range(n_side):
            copy = pltpu.make_async_copy(
                side.at[phase, b],
                grid_ref.at[pl.ds(at, nb), lead + b * nb : lead + b * nb + nb],
                sems.at[len(lead_copies) + len(side_copies)],
            )
            side_copies.append((True, copy))
    if phase:
        copy = pltpu.make_async_copy(
            old, grid_ref.at[:c0, c0:], sems.at[len(lead_copies) + len(side_copies)]
        )
        lead_copies.append((True, copy))
    always = cols_dev == STEPS
    for wanted, copy in lead_copies + side_copies:
        guarded(always or wanted is True, wanted, copy.start)
    if phase:
        col_ref[:c0, :] = old_col[...]
        col_ref[c0:, :] = jnp.zeros((lead - c0, nb), F32)
        top[...] = old_top[...]
    else:
        col_ref[...] = jnp.zeros(col_ref.shape, F32)
        top[...] = jnp.zeros(top.shape, F32)
    for wanted, copy in lead_copies:
        guarded(always or wanted is True, wanted, copy.wait)

    def pending(i, first_col):
        at = slice(i * nb, i * nb + nb)
        off = first_col - c0
        grid_ref[at, first_col:] = grid_ref[at, first_col:] - three(
            (lcol[0, at, :], lcol[1, at, :]), (rrow[0, :, off:], rrow[1, :, off:]), MM
        )

    def schur(turn):
        if turn == 0:
            upper[0], upper[1] = split2(grid_ref[:c0, c0:])
        elif turn <= rows_dev:
            at = slice(c0 + (turn - 1) * nb, c0 + turn * nb)
            grid_ref[at, c0:] = grid_ref[at, c0:] - three(
                split2(grid_ref[at, :c0]), (upper[0], upper[1]), MM
            )

    def settle(k, here):
        base = k * nb
        g = held[...]
        r = three(split2(gram(g, g)), split2(grid_ref[here, c0:]), MM)
        at = lax.broadcasted_iota(jnp.int32, (rows, nb), 0)
        column = jnp.where((at >= base) & (at < base + nb), 0.0, grid_ref[:rows, here])
        lcol[0], lcol[1] = split2(column)
        rrow[0], rrow[1] = split2(r)
        grid_ref[here, c0:] = r

    def step(k, here, filler):
        base = k * nb
        tile[:, nb:] = eye
        factor_tile(tile, nb, filler)
        held[...] = tile[:, nb:]

        @pl.when(k == my_col)
        def _():
            g = held[...]
            gs = split2(g)
            for a in range(na):
                row = a * rows_dev + my_row

                @pl.when(row == k)
                def _():
                    top[a] = jnp.where(ii >= jj, tile[:, :nb].T, 0.0)

                @pl.when(row > k)
                def _():
                    block = grid_ref[here, pl.ds(pl.multiple_of(row * nb, nb), nb)]
                    top[a] = three(gs, split2(block), MM).T

            at = lax.broadcasted_iota(jnp.int32, (rows, nb), 0)
            found = three(split2(grid_ref[:rows, here]), gs, ((1,), (1,)))
            col_ref[:rows, :] = jnp.where(at < base, -found, 0.0)
            col_ref[here, :] = g.T

    here = slice(c0, c0 + nb)
    if phase:
        for wanted, copy in side_copies:
            copy.wait()
        tile[:, :nb] = grid_ref[here, here] - three(
            split2(grid_ref[here, :c0]), split2(grid_ref[:c0, here]), MM
        )
        step(phase * rows_dev, here, schur)
    else:
        tile[:, :nb] = grid_ref[here, here]

        def arrive(turn):
            if turn == nb // PANEL - 1:
                for wanted, copy in side_copies:
                    copy.wait()

        step(0, here, arrive)

    @pl.loop(phase * rows_dev + 1, (phase + 1) * rows_dev)
    def _(k):
        before = pl.ds(pl.multiple_of(k * nb - nb, nb), nb)
        here = pl.ds(pl.multiple_of(k * nb, nb), nb)
        cross = three(split2(held[...]), split2(grid_ref[before, here]), MM)
        tile[:, :nb] = grid_ref[here, here] - three(split2(cross), split2(cross), ((0,), (0,)))

        def late(turn):
            if turn == 0:
                settle(k - 1, before)
            turns = nb // PANEL - 1
            for i in range(rows // nb):
                if i % turns == turn - 1:
                    pending(i, c0)

        step(k, here, late)

    settle((phase + 1) * rows_dev - 1, slice(rows - nb, rows))
    sent = []
    for i in range(rows // nb):
        at = slice(i * nb, i * nb + nb)
        if last:
            pending(i, lead)
            first = col_ref[at, :]
            if not fwd:
                first = jnp.where(my_col < STEPS, first, grid_ref[at, lead : lead + nb])
            solved_buf[0, at, :nb], solved_buf[1, at, :nb] = split2(first)
            solved_buf[0, at, nb:], solved_buf[1, at, nb:] = split2(
                grid_ref[at, lead + (nb if not fwd else 0) :]
            )
            copy = pltpu.make_async_copy(solved_buf.at[:, at, :], solved.at[:, at, :], out_sems.at[i])
        else:
            pending(i, rows)
            copy = pltpu.make_async_copy(grid_ref.at[at, rows:], passed.at[at, :], out_sems.at[i])
        copy.start()
        sent.append(copy)
    for copy in sent:
        copy.wait()


def close_kernel(place, *refs, nb, na, block_rows, block_cols, cols_dev, n_low):
    n_high = cols_dev // n_low
    near = refs[:n_high]
    far0, far, mine, solved, top, out = refs[n_high : n_high + 6]
    raw, old, right, left_h, left_m, made, sems, out_sems = refs[n_high + 6 :]
    my_col = place[1]
    MM = ((1,), (0,))
    always = cols_dev == STEPS
    group = nb * block_cols
    loads = []
    for back_l in range(n_low):
        for back_h in range(n_high):
            n = back_l * n_high + back_h
            across = near[back_h] if back_l == 0 else far0 if back_h == 0 else far.at[back_h - 1]
            col = col_of(my_col, back_h, back_l, cols_dev, n_low)
            copy = pltpu.make_async_copy(across, raw.at[n], sems.at[n])
            guarded(always, col < STEPS, copy.start)
            loads.append((n, col, copy))
    right_copy = pltpu.make_async_copy(solved, right, sems.at[cols_dev])
    right_copy.start()
    old_copy = pltpu.make_async_copy(mine.at[na * group :, :], old, sems.at[cols_dev + 1])
    old_copy.start()

    sent = []

    def send(a):
        at = slice(a * group, a * group + group)
        copy = pltpu.make_async_copy(made.at[at, :], out.at[at, :], out_sems.at[a])
        copy.start()
        sent.append(copy)

    for a in range(na):
        made[a * group : a * group + group, :] = jnp.zeros((group, nb), F32)
        made[pl.ds(a * group, nb, stride=block_cols), :] = top[a]
        send(a)
    for n, col, copy in loads:

        def take():
            copy.wait()
            at = pl.ds(pl.multiple_of(col * nb, nb), nb)
            left_h[:, at], left_m[:, at] = split2(raw[n])

        guarded(always, col < STEPS, take)
    right_copy.wait()
    old_copy.wait()
    is_panel = my_col < STEPS
    below = block_rows - na
    chunk = 3 if below % 3 == 0 else 1
    for first in range(0, below, chunk):
        at = slice(first * nb, (first + chunk) * nb)
        prod = three((left_h[at, :], left_m[at, :]), (right[0], right[1]), MM)
        for i in range(chunk):
            for b in range(block_cols):
                part = prod[i * nb : (i + 1) * nb, b * nb : (b + 1) * nb]
                prior = old[pl.ds((first + i) * group + b, nb, stride=block_cols), :]
                value = prior - part
                if b == 0:
                    value = jnp.where(is_panel, part, value)
                made[pl.ds((first + i + na) * group + b, nb, stride=block_cols), :] = value
            send(first + i + na)
    for copy in sent:
        copy.wait()


def local(matrix):
    rows_dev = lax.axis_size("row")
    cols_dev = lax.axis_size("col")
    my_row = lax.axis_index("row")
    my_col = lax.axis_index("col")
    block_rows, nb, block_cols, _ = matrix.shape
    na = STEPS // rows_dev
    fwd = STEPS // cols_dev
    lead = STEPS * nb
    wide = block_cols * nb
    n_side = block_cols - fwd
    n_low = 2
    n_high = cols_dev // n_low
    place = jnp.stack([my_row, my_col]).astype(jnp.int32)

    def tie(x, *after):
        return lax.optimization_barrier((x,) + after)[0] if after else x

    def step_to(x, axis, size, low, back_high, back_low):
        pairs = []
        for i in range(size):
            high, rest = divmod(i, low)
            pairs.append((i, (high + back_high) % (size // low) * low + (rest + back_low) % low))
        return lax.ppermute(x, axis, pairs)

    def line_of(x, *after):
        x = tie(x, *after)
        return [x] + [step_to(x, "col", cols_dev, n_low, h, 0) for h in range(1, n_high)]

    def across_rows(x, *after):
        x = tie(x, *after)
        return [x] + [step_to(x, "row", rows_dev, 2, h, 0) for h in range(1, rows_dev // 2)]

    def swap_core(x):
        return step_to(x, "row", rows_dev, 2, 0, 1)

    blocks = [matrix[a, :, 0, :] for a in range(na)]
    lines = [line_of(blocks[0])]
    side = across_rows(matrix[:na, :, fwd:, :].transpose(0, 2, 1, 3))
    strips = []
    for a in range(na):
        if a:
            lines.append(line_of(blocks[a], line))
        line = jnp.stack(lines[a])
        strips.append(jnp.concatenate([line, step_to(line, "col", cols_dev, n_low, 0, 1)]))
    body = line_of(matrix[na:, :, 0, :].reshape(-1, nb), strips[0])
    side = side + [swap_core(x) for x in side]
    body_far = step_to(tie(body[0], strips[0]), "col", cols_dev, n_low, 0, 1)
    phases = []
    for a in range(na):
        near = across_rows(strips[a], *(phases[0][1 : rows_dev // 2] if a else ()))
        phases.append(near + [swap_core(x) for x in near])

    vmem = pl.BlockSpec(memory_space=pltpu.VMEM)
    smem = pl.BlockSpec(memory_space=pltpu.SMEM)
    hbm = pl.BlockSpec(memory_space=pl.ANY)
    params = pltpu.CompilerParams(vmem_limit_bytes=56 << 20)
    carried = []
    for phase, pieces in enumerate(phases):
        last = phase == na - 1
        c0 = phase * rows_dev * nb
        rows = c0 + rows_dev * nb
        width = lead + n_side * nb
        out_shape = [jax.ShapeDtypeStruct((na, nb, nb), F32)]
        if last:
            out_shape = [jax.ShapeDtypeStruct((2, lead, wide), BF16)] + out_shape
        else:
            out_shape = [
                jax.ShapeDtypeStruct((rows, width - rows), F32),
                jax.ShapeDtypeStruct((rows, nb), F32),
            ] + out_shape
        carried = pl.pallas_call(
            functools.partial(
                sweep_kernel,
                phase=phase,
                last=last,
                nb=nb,
                na=na,
                rows_dev=rows_dev,
                cols_dev=cols_dev,
                fwd=fwd,
                n_pieces=len(pieces),
                n_low=n_low,
            ),
            out_shape=out_shape,
            in_specs=[smem] + [hbm] * (2 * len(pieces)) + ([hbm, vmem, vmem] if phase else []),
            out_specs=[hbm] + [vmem] * (len(out_shape) - 1),
            scratch_shapes=(
                [pltpu.VMEM((2, lead, wide), BF16), pltpu.VMEM((lead, nb), F32)] if last else []
            )
            + [
                pltpu.VMEM((rows, width), F32),
                pltpu.VMEM((nb, 2 * nb), F32),
                pltpu.VMEM((nb, nb), F32),
                pltpu.VMEM((2, rows, nb), BF16),
                pltpu.VMEM((2, nb, width - c0), BF16),
                pltpu.VMEM((2, max(c0, nb), width - c0), BF16),
                pltpu.SemaphoreType.DMA((len(pieces) * (cols_dev + n_side) + 1,)),
                pltpu.SemaphoreType.DMA((rows // nb,)),
            ],
            compiler_params=params,
            cost_estimate=pl.CostEstimate(flops=8 * 10**9, bytes_accessed=10**7, transcendentals=0),
            name="sweep%d" % phase,
        )(place, *pieces, *side, *carried)
        if phase == 0:
            far = step_to(jnp.stack([tie(x, carried[0]) for x in body[1:]]), "col", cols_dev, n_low, 0, 1)
    solved, top = carried
    out = pl.pallas_call(
        functools.partial(close_kernel, nb=nb, na=na, block_rows=block_rows, block_cols=block_cols, cols_dev=cols_dev, n_low=n_low),
        out_shape=jax.ShapeDtypeStruct((block_rows * nb * block_cols, nb), F32),
        in_specs=[smem] + [hbm] * (n_high + 4) + [vmem],
        out_specs=hbm,
        scratch_shapes=[
            pltpu.VMEM((cols_dev, (block_rows - na) * nb, nb), F32),
            pltpu.VMEM(((block_rows - na) * nb * block_cols, nb), F32),
            pltpu.VMEM((2, lead, wide), BF16),
            pltpu.VMEM(((block_rows - na) * nb, lead), BF16),
            pltpu.VMEM(((block_rows - na) * nb, lead), BF16),
            pltpu.VMEM((block_rows * nb * block_cols, nb), F32),
            pltpu.SemaphoreType.DMA((cols_dev + 2,)),
            pltpu.SemaphoreType.DMA((block_rows,)),
        ],
        compiler_params=params,
        name="close",
    )(place, *body, body_far, far, matrix.reshape(-1, nb), solved, top)
    return out.reshape(matrix.shape)


def solution(mesh):
    placed = (P(None, "row", None, "col"),)
    return jax.shard_map(
        local, mesh=mesh, in_specs=placed, out_specs=P(None, "row", None, "col"), check_vma=False
    )
```

```python
import functools

import jax
import jax.numpy as jnp
from jax import lax
from jax.experimental import pallas as pl
from jax.experimental.pallas import tpu as pltpu
from jax.sharding import PartitionSpec as P

STEPS = 8
PANEL = 32
SUB = 8
F32 = jnp.float32
BF16 = jnp.bfloat16


def split2(x):
    high = x.astype(BF16)
    return high, (x - high.astype(F32)).astype(BF16)


def split3(x):
    high = x.astype(BF16)
    rest = x - high.astype(F32)
    mid = rest.astype(BF16)
    return high, mid, (rest - mid.astype(F32)).astype(BF16)


def contract(left, right, dims):
    return lax.dot_general(left, right, (dims, ((), ())), preferred_element_type=F32)


def gram(rows_in, rows_wide):
    h, m, l = split3(rows_in)
    hw, mw, lw = split3(rows_wide)
    left = jnp.concatenate([h, h, m, m, h, l], 0)
    right = jnp.concatenate([hw, mw, hw, mw, lw, hw], 0)
    return contract(left, right, ((0,), (0,)))


def three(left, right, dims):
    (lh, lm), (rh, rm) = left, right
    return contract(lh, rh, dims) + (contract(lh, rm, dims) + contract(lm, rh, dims))


def factor_tile(tile, nb, filler):
    lane = lax.broadcasted_iota(jnp.int32, (SUB, nb), 1)
    sub = lax.broadcasted_iota(jnp.int32, (SUB, nb), 0)
    count = PANEL // SUB
    for first in range(0, nb, PANEL):
        after = first + PANEL
        parts = [tile[first + SUB * v : first + SUB * v + SUB, :] for v in range(count)]
        for b in range(count):
            at = first + SUB * b
            inside = (lane >= at) & (lane < at + SUB)
            row = [jnp.broadcast_to(parts[b][i : i + 1, :], (SUB, nb)) for i in range(SUB)]
            entry = {}
            for i in range(SUB):
                for s in range(i + 1):
                    entry[i, s] = jnp.broadcast_to(row[s][:, at + i : at + i + 1], (SUB, nb))
            below = [
                [jnp.broadcast_to(parts[v][:, at + t : at + t + 1], (SUB, nb)) for t in range(SUB)]
                for v in range(b + 1, count)
            ]
            row = [
                jnp.where(inside, jnp.where(lane == at + i, 1.0, 0.0), row[i]) for i in range(SUB)
            ]
            for s in range(SUB):
                scale = lax.rsqrt(entry[s, s])
                row[s] = row[s] * scale
                for column in below:
                    column[s] = column[s] * scale
                for i in range(s + 1, SUB):
                    entry[i, s] = entry[i, s] * scale
                for i in range(s + 1, SUB):
                    for t in range(s + 1, i + 1):
                        entry[i, t] = entry[i, t] - entry[i, s] * entry[t, s]
                for i in range(s + 1, SUB):
                    row[i] = row[i] - entry[i, s] * row[s]
                for column in below:
                    for t in range(s + 1, SUB):
                        column[t] = column[t] - column[s] * entry[t, s]
            made = row[0]
            for s in range(1, SUB):
                made = jnp.where(sub == s, row[s], made)
            for v, column in zip(range(b + 1, count), below):
                terms = [column[s] * row[s] for s in range(SUB)]
                while len(terms) > 1:
                    terms = [terms[n] + terms[n + 1] for n in range(0, len(terms), 2)]
                parts[v] = jnp.where(inside, 0.0, parts[v]) - terms[0]
            parts[b] = jnp.where((lane >= at + SUB) & (lane < after), 0.0, made)
            filler((first + SUB * b) // SUB)
        done = jnp.concatenate(parts, 0)
        tile[first:after, :] = done
        if after < nb:
            kept = lax.broadcasted_iota(jnp.int32, (nb - after, nb), 1)
            kept = (kept < first) | (kept >= after)
            tile[after:, :] = jnp.where(kept, tile[after:, :], 0.0) - gram(done, done)[after:, :]


def col_of(my_col, back_h, back_l, cols_dev, n_low):
    n_high = cols_dev // n_low
    high = lax.rem(my_col // n_low - back_h + n_high, n_high)
    return high * n_low + lax.rem(lax.rem(my_col, n_low) - back_l + n_low, n_low)


def guarded(always, condition, action):
    if always:
        action()
    else:
        pl.when(condition)(action)


def sweep_kernel(*refs, phase, last, nb, na, rows_dev, cols_dev, fwd, n_pieces, n_low):
    place = refs[0]
    pieces = refs[1 : 1 + n_pieces]
    sides = refs[1 + n_pieces : 1 + 2 * n_pieces]
    refs = refs[1 + 2 * n_pieces :]
    if phase:
        old, old_col, old_top = refs[:3]
        refs = refs[3:]
    if last:
        solved, top, solved_buf, col_ref = refs[:4]
        refs = refs[4:]
    else:
        passed, col_ref, top = refs[:3]
        refs = refs[3:]
    grid_ref, tile, held, origin, lcol, rrow, upper, sems, out_sems = refs
    my_row, my_col = place[0], place[1]
    lead = STEPS * nb
    c0 = phase * rows_dev * nb
    rows = c0 + rows_dev * nb
    n_side = sides[0].shape[1]
    ii = lax.broadcasted_iota(jnp.int32, (nb, nb), 0)
    jj = lax.broadcasted_iota(jnp.int32, (nb, nb), 1)
    MM = ((1,), (0,))

    lead_copies = []
    side_copies = []
    n_high = cols_dev // n_low
    for array, side, (back_hi, back_lo) in zip(
        pieces, sides, [(h, l) for l in range(2) for h in range(rows_dev // 2)], strict=True
    ):
        row_hi = lax.rem(my_row // 2 - back_hi + rows_dev // 2, rows_dev // 2)
        row_lo = lax.rem(lax.rem(my_row, 2) + back_lo, 2)
        at = pl.multiple_of(c0 + (row_hi * 2 + row_lo) * nb, nb)
        for i in range(cols_dev):
            col = col_of(my_col, i % n_high, i // n_high, cols_dev, n_low)
            copy = pltpu.make_async_copy(
                array.at[i],
                grid_ref.at[pl.ds(at, nb), pl.ds(pl.multiple_of(col * nb, nb), nb)],
                sems.at[len(lead_copies) + len(side_copies)],
            )
            lead_copies.append((col < STEPS, copy))
        for b in range(n_side):
            copy = pltpu.make_async_copy(
                side.at[phase, b],
                grid_ref.at[pl.ds(at, nb), lead + b * nb : lead + b * nb + nb],
                sems.at[len(lead_copies) + len(side_copies)],
            )
            side_copies.append((True, copy))
    if phase:
        copy = pltpu.make_async_copy(
            old, grid_ref.at[:c0, c0:], sems.at[len(lead_copies) + len(side_copies)]
        )
        lead_copies.append((True, copy))
    always = cols_dev == STEPS
    for wanted, copy in lead_copies + side_copies:
        guarded(always or wanted is True, wanted, copy.start)
    if phase:
        col_ref[:c0, :] = old_col[...]
        col_ref[c0:, :] = jnp.zeros((lead - c0, nb), F32)
        top[...] = old_top[...]
    else:
        col_ref[...] = jnp.zeros(col_ref.shape, F32)
        top[...] = jnp.zeros(top.shape, F32)
    for wanted, copy in lead_copies:
        guarded(always or wanted is True, wanted, copy.wait)

    def pending(i, first_col):
        at = slice(i * nb, i * nb + nb)
        off = first_col - c0
        grid_ref[at, first_col:] = grid_ref[at, first_col:] - three(
            (lcol[0, at, :], lcol[1, at, :]), (rrow[0, :, off:], rrow[1, :, off:]), MM
        )

    def schur(turn):
        if turn == 0:
            upper[0], upper[1] = split2(grid_ref[:c0, c0:])
        elif turn <= rows_dev:
            at = slice(c0 + (turn - 1) * nb, c0 + turn * nb)
            grid_ref[at, c0:] = grid_ref[at, c0:] - three(
                split2(grid_ref[at, :c0]), (upper[0], upper[1]), MM
            )

    def settle(k, here):
        base = k * nb
        g = held[...]
        r = three(split2(gram(g, g)), split2(grid_ref[here, c0:]), MM)
        at = lax.broadcasted_iota(jnp.int32, (rows, nb), 0)
        column = jnp.where((at >= base) & (at < base + nb), 0.0, grid_ref[:rows, here])
        lcol[0], lcol[1] = split2(column)
        rrow[0], rrow[1] = split2(r)
        grid_ref[here, c0:] = r

    def step(k, here, filler):
        base = k * nb
        origin[...] = tile[...]
        factor_tile(tile, nb, filler)
        held[...] = jnp.where(ii >= jj, tile[...], 0.0)

        @pl.when(k == my_col)
        def _():
            g = held[...]
            gs = split2(g)
            for a in range(na):
                row = a * rows_dev + my_row

                @pl.when(row == k)
                def _():
                    own = three(split2(origin[...]), gs, ((1,), (1,)))
                    top[a] = jnp.where(ii >= jj, own, 0.0)

                @pl.when(row > k)
                def _():
                    block = grid_ref[here, pl.ds(pl.multiple_of(row * nb, nb), nb)]
                    top[a] = three(gs, split2(block), MM).T

            at = lax.broadcasted_iota(jnp.int32, (rows, nb), 0)
            found = three(split2(grid_ref[:rows, here]), gs, ((1,), (1,)))
            col_ref[:rows, :] = jnp.where(at < base, -found, 0.0)
            col_ref[here, :] = g.T

    here = slice(c0, c0 + nb)
    if phase:
        for wanted, copy in side_copies:
            copy.wait()
        tile[...] = grid_ref[here, here] - three(
            split2(grid_ref[here, :c0]), split2(grid_ref[:c0, here]), MM
        )
        step(phase * rows_dev, here, schur)
    else:
        tile[...] = grid_ref[here, here]

        def arrive(turn):
            if turn == nb // SUB - 1:
                for wanted, copy in side_copies:
                    copy.wait()

        step(0, here, arrive)

    @pl.loop(phase * rows_dev + 1, (phase + 1) * rows_dev)
    def _(k):
        before = pl.ds(pl.multiple_of(k * nb - nb, nb), nb)
        here = pl.ds(pl.multiple_of(k * nb, nb), nb)
        cross = three(split2(held[...]), split2(grid_ref[before, here]), MM)
        tile[...] = grid_ref[here, here] - three(split2(cross), split2(cross), ((0,), (0,)))

        def late(turn):
            if turn == 0:
                settle(k - 1, before)
            turns = nb // SUB - 1
            for i in range(rows // nb):
                if i % turns == turn - 1:
                    pending(i, c0)

        step(k, here, late)

    settle((phase + 1) * rows_dev - 1, slice(rows - nb, rows))
    sent = []
    for i in range(rows // nb):
        at = slice(i * nb, i * nb + nb)
        if last:
            pending(i, lead)
            first = col_ref[at, :]
            if not fwd:
                first = jnp.where(my_col < STEPS, first, grid_ref[at, lead : lead + nb])
            solved_buf[0, at, :nb], solved_buf[1, at, :nb] = split2(first)
            solved_buf[0, at, nb:], solved_buf[1, at, nb:] = split2(
                grid_ref[at, lead + (nb if not fwd else 0) :]
            )
            copy = pltpu.make_async_copy(solved_buf.at[:, at, :], solved.at[:, at, :], out_sems.at[i])
        else:
            pending(i, rows)
            copy = pltpu.make_async_copy(grid_ref.at[at, rows:], passed.at[at, :], out_sems.at[i])
        copy.start()
        sent.append(copy)
    for copy in sent:
        copy.wait()


def close_kernel(place, *refs, nb, na, block_rows, block_cols, cols_dev, n_low):
    n_high = cols_dev // n_low
    near = refs[:n_high]
    far0, far, mine, solved, top, out = refs[n_high : n_high + 6]
    raw, old, right, left_h, left_m, made, sems, out_sems = refs[n_high + 6 :]
    my_col = place[1]
    MM = ((1,), (0,))
    always = cols_dev == STEPS
    group = nb * block_cols
    loads = []
    for back_l in range(n_low):
        for back_h in range(n_high):
            n = back_l * n_high + back_h
            across = near[back_h] if back_l == 0 else far0 if back_h == 0 else far.at[back_h - 1]
            col = col_of(my_col, back_h, back_l, cols_dev, n_low)
            copy = pltpu.make_async_copy(across, raw.at[n], sems.at[n])
            guarded(always, col < STEPS, copy.start)
            loads.append((n, col, copy))
    right_copy = pltpu.make_async_copy(solved, right, sems.at[cols_dev])
    right_copy.start()
    old_copy = pltpu.make_async_copy(mine.at[na * group :, :], old, sems.at[cols_dev + 1])
    old_copy.start()

    sent = []

    def send(a):
        at = slice(a * group, a * group + group)
        copy = pltpu.make_async_copy(made.at[at, :], out.at[at, :], out_sems.at[a])
        copy.start()
        sent.append(copy)

    for a in range(na):
        made[a * group : a * group + group, :] = jnp.zeros((group, nb), F32)
        made[pl.ds(a * group, nb, stride=block_cols), :] = top[a]
        send(a)
    for n, col, copy in loads:

        def take():
            copy.wait()
            at = pl.ds(pl.multiple_of(col * nb, nb), nb)
            left_h[:, at], left_m[:, at] = split2(raw[n])

        guarded(always, col < STEPS, take)
    right_copy.wait()
    old_copy.wait()
    is_panel = my_col < STEPS
    below = block_rows - na
    chunk = 3 if below % 3 == 0 else 1
    for first in range(0, below, chunk):
        at = slice(first * nb, (first + chunk) * nb)
        prod = three((left_h[at, :], left_m[at, :]), (right[0], right[1]), MM)
        for i in range(chunk):
            for b in range(block_cols):
                part = prod[i * nb : (i + 1) * nb, b * nb : (b + 1) * nb]
                prior = old[pl.ds((first + i) * group + b, nb, stride=block_cols), :]
                value = prior - part
                if b == 0:
                    value = jnp.where(is_panel, part, value)
                made[pl.ds((first + i + na) * group + b, nb, stride=block_cols), :] = value
            send(first + i + na)
    for copy in sent:
        copy.wait()


def local(matrix):
    rows_dev = lax.axis_size("row")
    cols_dev = lax.axis_size("col")
    my_row = lax.axis_index("row")
    my_col = lax.axis_index("col")
    block_rows, nb, block_cols, _ = matrix.shape
    na = STEPS // rows_dev
    fwd = STEPS // cols_dev
    lead = STEPS * nb
    wide = block_cols * nb
    n_side = block_cols - fwd
    n_low = 2
    n_high = cols_dev // n_low
    place = jnp.stack([my_row, my_col]).astype(jnp.int32)

    def tie(x, *after):
        return lax.optimization_barrier((x,) + after)[0] if after else x

    def step_to(x, axis, size, low, back_high, back_low):
        pairs = []
        for i in range(size):
            high, rest = divmod(i, low)
            pairs.append((i, (high + back_high) % (size // low) * low + (rest + back_low) % low))
        return lax.ppermute(x, axis, pairs)

    def line_of(x, *after):
        x = tie(x, *after)
        return [x] + [step_to(x, "col", cols_dev, n_low, h, 0) for h in range(1, n_high)]

    def across_rows(x, *after):
        x = tie(x, *after)
        return [x] + [step_to(x, "row", rows_dev, 2, h, 0) for h in range(1, rows_dev // 2)]

    def swap_core(x):
        return step_to(x, "row", rows_dev, 2, 0, 1)

    blocks = [matrix[a, :, 0, :] for a in range(na)]
    lines = [line_of(blocks[0])]
    side = across_rows(matrix[:na, :, fwd:, :].transpose(0, 2, 1, 3))
    strips = []
    for a in range(na):
        if a:
            lines.append(line_of(blocks[a], line))
        line = jnp.stack(lines[a])
        strips.append(jnp.concatenate([line, step_to(line, "col", cols_dev, n_low, 0, 1)]))
    body = line_of(matrix[na:, :, 0, :].reshape(-1, nb), strips[0])
    side = side + [swap_core(x) for x in side]
    body_far = step_to(tie(body[0], strips[0]), "col", cols_dev, n_low, 0, 1)
    phases = []
    for a in range(na):
        near = across_rows(strips[a], *(phases[0][1 : rows_dev // 2] if a else ()))
        phases.append(near + [swap_core(x) for x in near])

    vmem = pl.BlockSpec(memory_space=pltpu.VMEM)
    smem = pl.BlockSpec(memory_space=pltpu.SMEM)
    hbm = pl.BlockSpec(memory_space=pl.ANY)
    params = pltpu.CompilerParams(vmem_limit_bytes=56 << 20)
    carried = []
    for phase, pieces in enumerate(phases):
        last = phase == na - 1
        c0 = phase * rows_dev * nb
        rows = c0 + rows_dev * nb
        width = lead + n_side * nb
        out_shape = [jax.ShapeDtypeStruct((na, nb, nb), F32)]
        if last:
            out_shape = [jax.ShapeDtypeStruct((2, lead, wide), BF16)] + out_shape
        else:
            out_shape = [
                jax.ShapeDtypeStruct((rows, width - rows), F32),
                jax.ShapeDtypeStruct((rows, nb), F32),
            ] + out_shape
        carried = pl.pallas_call(
            functools.partial(
                sweep_kernel,
                phase=phase,
                last=last,
                nb=nb,
                na=na,
                rows_dev=rows_dev,
                cols_dev=cols_dev,
                fwd=fwd,
                n_pieces=len(pieces),
                n_low=n_low,
            ),
            out_shape=out_shape,
            in_specs=[smem] + [hbm] * (2 * len(pieces)) + ([hbm, vmem, vmem] if phase else []),
            out_specs=[hbm] + [vmem] * (len(out_shape) - 1),
            scratch_shapes=(
                [pltpu.VMEM((2, lead, wide), BF16), pltpu.VMEM((lead, nb), F32)] if last else []
            )
            + [
                pltpu.VMEM((rows, width), F32),
                pltpu.VMEM((nb, nb), F32),
                pltpu.VMEM((nb, nb), F32),
                pltpu.VMEM((nb, nb), F32),
                pltpu.VMEM((2, rows, nb), BF16),
                pltpu.VMEM((2, nb, width - c0), BF16),
                pltpu.VMEM((2, max(c0, nb), width - c0), BF16),
                pltpu.SemaphoreType.DMA((len(pieces) * (cols_dev + n_side) + 1,)),
                pltpu.SemaphoreType.DMA((rows // nb,)),
            ],
            compiler_params=params,
            cost_estimate=pl.CostEstimate(flops=8 * 10**9, bytes_accessed=10**7, transcendentals=0),
            name="sweep%d" % phase,
        )(place, *pieces, *side, *carried)
        if phase == 0:
            far = step_to(jnp.stack([tie(x, carried[0], body_far) for x in body[1:]]), "col", cols_dev, n_low, 0, 1)
    solved, top = carried
    out = pl.pallas_call(
        functools.partial(close_kernel, nb=nb, na=na, block_rows=block_rows, block_cols=block_cols, cols_dev=cols_dev, n_low=n_low),
        out_shape=jax.ShapeDtypeStruct((block_rows * nb * block_cols, nb), F32),
        in_specs=[smem] + [hbm] * (n_high + 4) + [vmem],
        out_specs=hbm,
        scratch_shapes=[
            pltpu.VMEM((cols_dev, (block_rows - na) * nb, nb), F32),
            pltpu.VMEM(((block_rows - na) * nb * block_cols, nb), F32),
            pltpu.VMEM((2, lead, wide), BF16),
            pltpu.VMEM(((block_rows - na) * nb, lead), BF16),
            pltpu.VMEM(((block_rows - na) * nb, lead), BF16),
            pltpu.VMEM((block_rows * nb * block_cols, nb), F32),
            pltpu.SemaphoreType.DMA((cols_dev + 2,)),
            pltpu.SemaphoreType.DMA((block_rows,)),
        ],
        compiler_params=params,
        name="close",
    )(place, *body, body_far, far, matrix.reshape(-1, nb), solved, top)
    return out.reshape(matrix.shape)


def solution(mesh):
    placed = (P(None, "row", None, "col"),)
    return jax.shard_map(
        local, mesh=mesh, in_specs=placed, out_specs=P(None, "row", None, "col"), check_vma=False
    )
```

```python
import functools

import jax
import jax.numpy as jnp
from jax import lax
from jax.experimental import pallas as pl
from jax.experimental.pallas import tpu as pltpu
from jax.sharding import PartitionSpec as P

STEPS = 8
PANEL = 32
SUB = 8
F32 = jnp.float32
BF16 = jnp.bfloat16


def split2(x):
    high = x.astype(BF16)
    return high, (x - high.astype(F32)).astype(BF16)


def split3(x):
    high = x.astype(BF16)
    rest = x - high.astype(F32)
    mid = rest.astype(BF16)
    return high, mid, (rest - mid.astype(F32)).astype(BF16)


def contract(left, right, dims):
    return lax.dot_general(left, right, (dims, ((), ())), preferred_element_type=F32)


def gram(rows_in, rows_wide):
    h, m, l = split3(rows_in)
    hw, mw, lw = split3(rows_wide)
    left = jnp.concatenate([h, h, m, m, h, l], 0)
    right = jnp.concatenate([hw, mw, hw, mw, lw, hw], 0)
    return contract(left, right, ((0,), (0,)))


def three(left, right, dims):
    (lh, lm), (rh, rm) = left, right
    return contract(lh, rh, dims) + (contract(lh, rm, dims) + contract(lm, rh, dims))


def factor_tile(tile, nb, filler):
    lane = lax.broadcasted_iota(jnp.int32, (SUB, nb), 1)
    sub = lax.broadcasted_iota(jnp.int32, (SUB, nb), 0)
    count = PANEL // SUB
    for first in range(0, nb, PANEL):
        after = first + PANEL
        parts = [tile[first + SUB * v : first + SUB * v + SUB, :] for v in range(count)]
        for b in range(count):
            at = first + SUB * b
            inside = (lane >= at) & (lane < at + SUB)
            row = [jnp.broadcast_to(parts[b][i : i + 1, :], (SUB, nb)) for i in range(SUB)]
            entry = {}
            for i in range(SUB):
                for s in range(i + 1):
                    entry[i, s] = jnp.broadcast_to(row[s][:, at + i : at + i + 1], (SUB, nb))
            below = [
                [jnp.broadcast_to(parts[v][:, at + t : at + t + 1], (SUB, nb)) for t in range(SUB)]
                for v in range(b + 1, count)
            ]
            row = [
                jnp.where(inside, jnp.where(lane == at + i, 1.0, 0.0), row[i]) for i in range(SUB)
            ]
            for s in range(SUB):
                scale = lax.rsqrt(entry[s, s])
                row[s] = row[s] * scale
                for column in below:
                    column[s] = column[s] * scale
                for i in range(s + 1, SUB):
                    entry[i, s] = entry[i, s] * scale
                for i in range(s + 1, SUB):
                    for t in range(s + 1, i + 1):
                        entry[i, t] = entry[i, t] - entry[i, s] * entry[t, s]
                for i in range(s + 1, SUB):
                    row[i] = row[i] - entry[i, s] * row[s]
                for column in below:
                    for t in range(s + 1, SUB):
                        column[t] = column[t] - column[s] * entry[t, s]
            made = row[0]
            for s in range(1, SUB):
                made = jnp.where(sub == s, row[s], made)
            for v, column in zip(range(b + 1, count), below):
                terms = [column[s] * row[s] for s in range(SUB)]
                while len(terms) > 1:
                    terms = [terms[n] + terms[n + 1] for n in range(0, len(terms), 2)]
                parts[v] = jnp.where(inside, 0.0, parts[v]) - terms[0]
            parts[b] = jnp.where((lane >= at + SUB) & (lane < after), 0.0, made)
            filler((first + SUB * b) // SUB)
        done = jnp.concatenate(parts, 0)
        tile[first:after, :] = done
        if after < nb:
            kept = lax.broadcasted_iota(jnp.int32, (nb - after, nb), 1)
            kept = (kept < first) | (kept >= after)
            tile[after:, :] = jnp.where(kept, tile[after:, :], 0.0) - gram(done, done)[after:, :]


def col_of(my_col, back_h, back_l, cols_dev, n_low):
    n_high = cols_dev // n_low
    high = lax.rem(my_col // n_low - back_h + n_high, n_high)
    return high * n_low + lax.rem(lax.rem(my_col, n_low) - back_l + n_low, n_low)


def guarded(always, condition, action):
    if always:
        action()
    else:
        pl.when(condition)(action)


def sweep_kernel(*refs, phase, last, nb, na, rows_dev, cols_dev, fwd, n_pieces, n_low):
    place = refs[0]
    pieces = refs[1 : 1 + n_pieces]
    sides = refs[1 + n_pieces : 1 + 2 * n_pieces]
    refs = refs[1 + 2 * n_pieces :]
    if phase:
        old, old_col, old_top = refs[:3]
        refs = refs[3:]
    if last:
        solved, top, solved_buf, col_ref = refs[:4]
        refs = refs[4:]
    else:
        passed, col_ref, top = refs[:3]
        refs = refs[3:]
    grid_ref, tile, held, origin, lcol, rrow, upper, sems, out_sems = refs
    my_row, my_col = place[0], place[1]
    lead = STEPS * nb
    c0 = phase * rows_dev * nb
    rows = c0 + rows_dev * nb
    n_side = sides[0].shape[1]
    ii = lax.broadcasted_iota(jnp.int32, (nb, nb), 0)
    jj = lax.broadcasted_iota(jnp.int32, (nb, nb), 1)
    MM = ((1,), (0,))

    lead_copies = []
    side_copies = []
    n_high = cols_dev // n_low
    for array, side, (back_hi, back_lo) in zip(
        pieces, sides, [(h, l) for l in range(2) for h in range(rows_dev // 2)], strict=True
    ):
        row_hi = lax.rem(my_row // 2 - back_hi + rows_dev // 2, rows_dev // 2)
        row_lo = lax.rem(lax.rem(my_row, 2) + back_lo, 2)
        at = pl.multiple_of(c0 + (row_hi * 2 + row_lo) * nb, nb)
        for i in range(cols_dev):
            col = col_of(my_col, i % n_high, i // n_high, cols_dev, n_low)
            copy = pltpu.make_async_copy(
                array.at[i],
                grid_ref.at[pl.ds(at, nb), pl.ds(pl.multiple_of(col * nb, nb), nb)],
                sems.at[len(lead_copies) + len(side_copies)],
            )
            lead_copies.append((col < STEPS, copy))
        for b in range(n_side):
            copy = pltpu.make_async_copy(
                side.at[phase, b],
                grid_ref.at[pl.ds(at, nb), lead + b * nb : lead + b * nb + nb],
                sems.at[len(lead_copies) + len(side_copies)],
            )
            side_copies.append((True, copy))
    if phase:
        copy = pltpu.make_async_copy(
            old, grid_ref.at[:c0, c0:], sems.at[len(lead_copies) + len(side_copies)]
        )
        lead_copies.append((True, copy))
    always = cols_dev == STEPS
    for wanted, copy in lead_copies + side_copies:
        guarded(always or wanted is True, wanted, copy.start)
    if phase:
        col_ref[:c0, :] = old_col[...]
        col_ref[c0:, :] = jnp.zeros((lead - c0, nb), F32)
        top[...] = old_top[...]
    else:
        col_ref[...] = jnp.zeros(col_ref.shape, F32)
        top[...] = jnp.zeros(top.shape, F32)
    for wanted, copy in lead_copies:
        guarded(always or wanted is True, wanted, copy.wait)

    def pending(i, first_col):
        at = slice(i * nb, i * nb + nb)
        off = first_col - c0
        grid_ref[at, first_col:] = grid_ref[at, first_col:] - three(
            (lcol[0, at, :], lcol[1, at, :]), (rrow[0, :, off:], rrow[1, :, off:]), MM
        )

    def schur(turn):
        if turn == 0:
            upper[0], upper[1] = split2(grid_ref[:c0, c0:])
        elif turn <= rows_dev:
            at = slice(c0 + (turn - 1) * nb, c0 + turn * nb)
            grid_ref[at, c0:] = grid_ref[at, c0:] - three(
                split2(grid_ref[at, :c0]), (upper[0], upper[1]), MM
            )

    def settle(k, here):
        base = k * nb
        g = held[...]
        r = three(split2(gram(g, g)), split2(grid_ref[here, c0:]), MM)
        at = lax.broadcasted_iota(jnp.int32, (rows, nb), 0)
        column = jnp.where((at >= base) & (at < base + nb), 0.0, grid_ref[:rows, here])
        lcol[0], lcol[1] = split2(column)
        rrow[0], rrow[1] = split2(r)
        grid_ref[here, c0:] = r

    def step(k, here, filler):
        base = k * nb
        origin[...] = tile[...]
        factor_tile(tile, nb, filler)
        held[...] = jnp.where(ii >= jj, tile[...], 0.0)

        @pl.when(k == my_col)
        def _():
            g = held[...]
            gs = split2(g)
            for a in range(na):
                row = a * rows_dev + my_row

                @pl.when(row == k)
                def _():
                    own = three(split2(origin[...]), gs, ((1,), (1,)))
                    top[a] = jnp.where(ii >= jj, own, 0.0)

                @pl.when(row > k)
                def _():
                    block = grid_ref[here, pl.ds(pl.multiple_of(row * nb, nb), nb)]
                    top[a] = three(gs, split2(block), MM).T

            at = lax.broadcasted_iota(jnp.int32, (rows, nb), 0)
            found = three(split2(grid_ref[:rows, here]), gs, ((1,), (1,)))
            col_ref[:rows, :] = jnp.where(at < base, -found, 0.0)
            col_ref[here, :] = g.T

    here = slice(c0, c0 + nb)
    if phase:
        for wanted, copy in side_copies:
            copy.wait()
        tile[...] = grid_ref[here, here] - three(
            split2(grid_ref[here, :c0]), split2(grid_ref[:c0, here]), MM
        )
        step(phase * rows_dev, here, schur)
    else:
        tile[...] = grid_ref[here, here]

        def arrive(turn):
            if turn == nb // SUB - 1:
                for wanted, copy in side_copies:
                    copy.wait()

        step(0, here, arrive)

    @pl.loop(phase * rows_dev + 1, (phase + 1) * rows_dev)
    def _(k):
        before = pl.ds(pl.multiple_of(k * nb - nb, nb), nb)
        here = pl.ds(pl.multiple_of(k * nb, nb), nb)
        cross = three(split2(held[...]), split2(grid_ref[before, here]), MM)
        tile[...] = grid_ref[here, here] - three(split2(cross), split2(cross), ((0,), (0,)))

        def late(turn):
            if turn == 0:
                settle(k - 1, before)
            turns = nb // SUB - 1
            for i in range(rows // nb):
                if i % turns == turn - 1:
                    pending(i, c0)

        step(k, here, late)

    settle((phase + 1) * rows_dev - 1, slice(rows - nb, rows))
    sent = []
    for i in range(rows // nb):
        at = slice(i * nb, i * nb + nb)
        if last:
            pending(i, lead)
            first = col_ref[at, :]
            if not fwd:
                first = jnp.where(my_col < STEPS, first, grid_ref[at, lead : lead + nb])
            solved_buf[0, at, :nb], solved_buf[1, at, :nb] = split2(first)
            solved_buf[0, at, nb:], solved_buf[1, at, nb:] = split2(
                grid_ref[at, lead + (nb if not fwd else 0) :]
            )
            copy = pltpu.make_async_copy(solved_buf.at[:, at, :], solved.at[:, at, :], out_sems.at[i])
        else:
            pending(i, rows)
            copy = pltpu.make_async_copy(grid_ref.at[at, rows:], passed.at[at, :], out_sems.at[i])
        copy.start()
        sent.append(copy)
    for copy in sent:
        copy.wait()


def close_kernel(place, *refs, nb, na, block_rows, block_cols, cols_dev, n_low):
    n_high = cols_dev // n_low
    near = refs[:n_high]
    far0, far, mine, solved, top, out = refs[n_high : n_high + 6]
    raw, old, right, left_h, left_m, made, sems, out_sems = refs[n_high + 6 :]
    my_col = place[1]
    MM = ((1,), (0,))
    always = cols_dev == STEPS
    group = nb * block_cols
    loads = []
    for back_l in range(n_low):
        for back_h in range(n_high):
            n = back_l * n_high + back_h
            across = near[back_h] if back_l == 0 else far0 if back_h == 0 else far.at[back_h - 1]
            col = col_of(my_col, back_h, back_l, cols_dev, n_low)
            copy = pltpu.make_async_copy(across, raw.at[n], sems.at[n])
            guarded(always, col < STEPS, copy.start)
            loads.append((n, col, copy))
    right_copy = pltpu.make_async_copy(solved, right, sems.at[cols_dev])
    right_copy.start()
    old_copy = pltpu.make_async_copy(mine.at[na * group :, :], old, sems.at[cols_dev + 1])
    old_copy.start()

    sent = []

    def send(a):
        at = slice(a * group, a * group + group)
        copy = pltpu.make_async_copy(made.at[at, :], out.at[at, :], out_sems.at[a])
        copy.start()
        sent.append(copy)

    for a in range(na):
        made[a * group : a * group + group, :] = jnp.zeros((group, nb), F32)
        made[pl.ds(a * group, nb, stride=block_cols), :] = top[a]
        send(a)
    for n, col, copy in loads:

        def take():
            copy.wait()
            at = pl.ds(pl.multiple_of(col * nb, nb), nb)
            left_h[:, at], left_m[:, at] = split2(raw[n])

        guarded(always, col < STEPS, take)
    right_copy.wait()
    old_copy.wait()
    is_panel = my_col < STEPS
    below = block_rows - na
    chunk = 3 if below % 3 == 0 else 1
    for first in range(0, below, chunk):
        at = slice(first * nb, (first + chunk) * nb)
        prod = three((left_h[at, :], left_m[at, :]), (right[0], right[1]), MM)
        for i in range(chunk):
            for b in range(block_cols):
                part = prod[i * nb : (i + 1) * nb, b * nb : (b + 1) * nb]
                prior = old[pl.ds((first + i) * group + b, nb, stride=block_cols), :]
                value = prior - part
                if b == 0:
                    value = jnp.where(is_panel, part, value)
                made[pl.ds((first + i + na) * group + b, nb, stride=block_cols), :] = value
            send(first + i + na)
    for copy in sent:
        copy.wait()


def local(matrix):
    rows_dev = lax.axis_size("row")
    cols_dev = lax.axis_size("col")
    my_row = lax.axis_index("row")
    my_col = lax.axis_index("col")
    block_rows, nb, block_cols, _ = matrix.shape
    na = STEPS // rows_dev
    fwd = STEPS // cols_dev
    lead = STEPS * nb
    wide = block_cols * nb
    n_side = block_cols - fwd
    n_low = 2
    n_high = cols_dev // n_low
    place = jnp.stack([my_row, my_col]).astype(jnp.int32)

    def tie(x, *after):
        return lax.optimization_barrier((x,) + after)[0] if after else x

    def step_to(x, axis, size, low, back_high, back_low):
        pairs = []
        for i in range(size):
            high, rest = divmod(i, low)
            pairs.append((i, (high + back_high) % (size // low) * low + (rest + back_low) % low))
        return lax.ppermute(x, axis, pairs)

    def line_of(x, *after):
        x = tie(x, *after)
        return [x] + [step_to(x, "col", cols_dev, n_low, h, 0) for h in range(1, n_high)]

    def across_rows(x, *after):
        x = tie(x, *after)
        return [x] + [step_to(x, "row", rows_dev, 2, h, 0) for h in range(1, rows_dev // 2)]

    def swap_core(x):
        return step_to(x, "row", rows_dev, 2, 0, 1)

    blocks = [matrix[a, :, 0, :] for a in range(na)]
    lines = [line_of(blocks[0])]
    side = across_rows(matrix[:na, :, fwd:, :].transpose(0, 2, 1, 3))
    strips = []
    for a in range(na):
        if a:
            lines.append(line_of(blocks[a], side[1]))
        line = jnp.stack(lines[a])
        strips.append(jnp.concatenate([line, step_to(line, "col", cols_dev, n_low, 0, 1)]))
    body = line_of(matrix[na:, :, 0, :].reshape(-1, nb), strips[0])
    side = side + [swap_core(x) for x in side]
    body_far = step_to(tie(body[0], strips[0]), "col", cols_dev, n_low, 0, 1)
    phases = []
    for a in range(na):
        near = across_rows(strips[a], *(phases[0][1 : rows_dev // 2] if a else ()))
        phases.append(near + [swap_core(x) for x in near])

    vmem = pl.BlockSpec(memory_space=pltpu.VMEM)
    smem = pl.BlockSpec(memory_space=pltpu.SMEM)
    hbm = pl.BlockSpec(memory_space=pl.ANY)
    params = pltpu.CompilerParams(vmem_limit_bytes=20 << 20)
    carried = []
    for phase, pieces in enumerate(phases):
        last = phase == na - 1
        c0 = phase * rows_dev * nb
        rows = c0 + rows_dev * nb
        width = lead + n_side * nb
        out_shape = [jax.ShapeDtypeStruct((na, nb, nb), F32)]
        if last:
            out_shape = [jax.ShapeDtypeStruct((2, lead, wide), BF16)] + out_shape
        else:
            out_shape = [
                jax.ShapeDtypeStruct((rows, width - rows), F32),
                jax.ShapeDtypeStruct((rows, nb), F32),
            ] + out_shape
        carried = pl.pallas_call(
            functools.partial(
                sweep_kernel,
                phase=phase,
                last=last,
                nb=nb,
                na=na,
                rows_dev=rows_dev,
                cols_dev=cols_dev,
                fwd=fwd,
                n_pieces=len(pieces),
                n_low=n_low,
            ),
            out_shape=out_shape,
            in_specs=[smem] + [hbm] * (2 * len(pieces)) + ([hbm, vmem, vmem] if phase else []),
            out_specs=[hbm] + [vmem] * (len(out_shape) - 1),
            scratch_shapes=(
                [pltpu.VMEM((2, lead, wide), BF16), pltpu.VMEM((lead, nb), F32)] if last else []
            )
            + [
                pltpu.VMEM((rows, width), F32),
                pltpu.VMEM((nb, nb), F32),
                pltpu.VMEM((nb, nb), F32),
                pltpu.VMEM((nb, nb), F32),
                pltpu.VMEM((2, rows, nb), BF16),
                pltpu.VMEM((2, nb, width - c0), BF16),
                pltpu.VMEM((2, max(c0, nb), width - c0), BF16),
                pltpu.SemaphoreType.DMA((len(pieces) * (cols_dev + n_side) + 1,)),
                pltpu.SemaphoreType.DMA((rows // nb,)),
            ],
            compiler_params=params,
            cost_estimate=pl.CostEstimate(flops=3 * 10**9, bytes_accessed=10**7, transcendentals=0),
            name="sweep%d" % phase,
        )(place, *pieces, *side, *carried)
        if phase == 0:
            far = step_to(jnp.stack([tie(x, carried[0], body_far) for x in body[1:]]), "col", cols_dev, n_low, 0, 1)
    solved, top = carried
    out = pl.pallas_call(
        functools.partial(close_kernel, nb=nb, na=na, block_rows=block_rows, block_cols=block_cols, cols_dev=cols_dev, n_low=n_low),
        out_shape=jax.ShapeDtypeStruct((block_rows * nb * block_cols, nb), F32),
        in_specs=[smem] + [hbm] * (n_high + 4) + [vmem],
        out_specs=hbm,
        scratch_shapes=[
            pltpu.VMEM((cols_dev, (block_rows - na) * nb, nb), F32),
            pltpu.VMEM(((block_rows - na) * nb * block_cols, nb), F32),
            pltpu.VMEM((2, lead, wide), BF16),
            pltpu.VMEM(((block_rows - na) * nb, lead), BF16),
            pltpu.VMEM(((block_rows - na) * nb, lead), BF16),
            pltpu.VMEM((block_rows * nb * block_cols, nb), F32),
            pltpu.SemaphoreType.DMA((cols_dev + 2,)),
            pltpu.SemaphoreType.DMA((block_rows,)),
        ],
        compiler_params=params,
        name="close",
    )(place, *body, body_far, far, matrix.reshape(-1, nb), solved, top)
    return out.reshape(matrix.shape)


def solution(mesh):
    placed = (P(None, "row", None, "col"),)
    return jax.shard_map(
        local, mesh=mesh, in_specs=placed, out_specs=P(None, "row", None, "col"), check_vma=False
    )
```

```python
import functools

import jax
import jax.numpy as jnp
from jax import lax
from jax.experimental import pallas as pl
from jax.experimental.pallas import tpu as pltpu
from jax.sharding import PartitionSpec as P

STEPS = 8
PANEL = 64
SUB = 8
F32 = jnp.float32
BF16 = jnp.bfloat16


def split2(x):
    high = x.astype(BF16)
    return high, (x - high.astype(F32)).astype(BF16)


def split3(x):
    high = x.astype(BF16)
    rest = x - high.astype(F32)
    mid = rest.astype(BF16)
    return high, mid, (rest - mid.astype(F32)).astype(BF16)


def contract(left, right, dims):
    return lax.dot_general(left, right, (dims, ((), ())), preferred_element_type=F32)


def gram(rows_in, rows_wide):
    h, m, l = split3(rows_in)
    hw, mw, lw = split3(rows_wide)
    left = jnp.concatenate([h, h, m, m, h, l], 0)
    right = jnp.concatenate([hw, mw, hw, mw, lw, hw], 0)
    return contract(left, right, ((0,), (0,)))


def three(left, right, dims):
    (lh, lm), (rh, rm) = left, right
    return contract(lh, rh, dims) + (contract(lh, rm, dims) + contract(lm, rh, dims))


def factor_tile(tile, nb, filler):
    lane = lax.broadcasted_iota(jnp.int32, (SUB, nb), 1)
    sub = lax.broadcasted_iota(jnp.int32, (SUB, nb), 0)
    count = PANEL // SUB
    for first in range(0, nb, PANEL):
        after = first + PANEL
        parts = [tile[first + SUB * v : first + SUB * v + SUB, :] for v in range(count)]
        for b in range(count):
            at = first + SUB * b
            inside = (lane >= at) & (lane < at + SUB)
            row = [jnp.broadcast_to(parts[b][i : i + 1, :], (SUB, nb)) for i in range(SUB)]
            entry = {}
            for i in range(SUB):
                for s in range(i + 1):
                    entry[i, s] = jnp.broadcast_to(row[s][:, at + i : at + i + 1], (SUB, nb))
            below = [
                [jnp.broadcast_to(parts[v][:, at + t : at + t + 1], (SUB, nb)) for t in range(SUB)]
                for v in range(b + 1, count)
            ]
            row = [
                jnp.where(inside, jnp.where(lane == at + i, 1.0, 0.0), row[i]) for i in range(SUB)
            ]
            for s in range(SUB):
                scale = lax.rsqrt(entry[s, s])
                row[s] = row[s] * scale
                for column in below:
                    column[s] = column[s] * scale
                for i in range(s + 1, SUB):
                    entry[i, s] = entry[i, s] * scale
                for i in range(s + 1, SUB):
                    for t in range(s + 1, i + 1):
                        entry[i, t] = entry[i, t] - entry[i, s] * entry[t, s]
                for i in range(s + 1, SUB):
                    row[i] = row[i] - entry[i, s] * row[s]
                for column in below:
                    for t in range(s + 1, SUB):
                        column[t] = column[t] - column[s] * entry[t, s]
            made = row[0]
            for s in range(1, SUB):
                made = jnp.where(sub == s, row[s], made)
            for v, column in zip(range(b + 1, count), below):
                terms = [column[s] * row[s] for s in range(SUB)]
                while len(terms) > 1:
                    terms = [terms[n] + terms[n + 1] for n in range(0, len(terms), 2)]
                parts[v] = jnp.where(inside, 0.0, parts[v]) - terms[0]
            parts[b] = jnp.where((lane >= at + SUB) & (lane < after), 0.0, made)
            filler((first + SUB * b) // SUB)
        done = jnp.concatenate(parts, 0)
        tile[first:after, :] = done
        if after < nb:
            kept = lax.broadcasted_iota(jnp.int32, (nb - after, nb), 1)
            kept = (kept < first) | (kept >= after)
            tile[after:, :] = jnp.where(kept, tile[after:, :], 0.0) - gram(done, done)[after:, :]


def col_of(my_col, back_h, back_l, cols_dev, n_low):
    n_high = cols_dev // n_low
    high = lax.rem(my_col // n_low - back_h + n_high, n_high)
    return high * n_low + lax.rem(lax.rem(my_col, n_low) - back_l + n_low, n_low)


def guarded(always, condition, action):
    if always:
        action()
    else:
        pl.when(condition)(action)


def sweep_kernel(*refs, phase, last, nb, na, rows_dev, cols_dev, fwd, n_pieces, n_low):
    place = refs[0]
    pieces = refs[1 : 1 + n_pieces]
    sides = refs[1 + n_pieces : 1 + 2 * n_pieces]
    refs = refs[1 + 2 * n_pieces :]
    if phase:
        old, old_col, old_top = refs[:3]
        refs = refs[3:]
    if last:
        solved, top, solved_buf, col_ref = refs[:4]
        refs = refs[4:]
    else:
        passed, col_ref, top = refs[:3]
        refs = refs[3:]
    grid_ref, tile, held, origin, lcol, rrow, upper, sems, out_sems = refs
    my_row, my_col = place[0], place[1]
    lead = STEPS * nb
    c0 = phase * rows_dev * nb
    rows = c0 + rows_dev * nb
    n_side = sides[0].shape[1]
    ii = lax.broadcasted_iota(jnp.int32, (nb, nb), 0)
    jj = lax.broadcasted_iota(jnp.int32, (nb, nb), 1)
    MM = ((1,), (0,))

    lead_copies = []
    side_copies = []
    n_high = cols_dev // n_low
    for array, side, (back_hi, back_lo) in zip(
        pieces, sides, [(h, l) for l in range(2) for h in range(rows_dev // 2)], strict=True
    ):
        row_hi = lax.rem(my_row // 2 - back_hi + rows_dev // 2, rows_dev // 2)
        row_lo = lax.rem(lax.rem(my_row, 2) + back_lo, 2)
        at = pl.multiple_of(c0 + (row_hi * 2 + row_lo) * nb, nb)
        for i in range(cols_dev):
            col = col_of(my_col, i % n_high, i // n_high, cols_dev, n_low)
            copy = pltpu.make_async_copy(
                array.at[i],
                grid_ref.at[pl.ds(at, nb), pl.ds(pl.multiple_of(col * nb, nb), nb)],
                sems.at[len(lead_copies) + len(side_copies)],
            )
            lead_copies.append((col < STEPS, copy))
        for b in range(n_side):
            copy = pltpu.make_async_copy(
                side.at[phase, b],
                grid_ref.at[pl.ds(at, nb), lead + b * nb : lead + b * nb + nb],
                sems.at[len(lead_copies) + len(side_copies)],
            )
            side_copies.append((True, copy))
    if phase:
        copy = pltpu.make_async_copy(
            old, grid_ref.at[:c0, c0:], sems.at[len(lead_copies) + len(side_copies)]
        )
        lead_copies.append((True, copy))
    always = cols_dev == STEPS
    for wanted, copy in lead_copies + side_copies:
        guarded(always or wanted is True, wanted, copy.start)
    if phase:
        col_ref[:c0, :] = old_col[...]
        col_ref[c0:, :] = jnp.zeros((lead - c0, nb), F32)
        top[...] = old_top[...]
    else:
        col_ref[...] = jnp.zeros(col_ref.shape, F32)
        top[...] = jnp.zeros(top.shape, F32)
    for wanted, copy in lead_copies:
        guarded(always or wanted is True, wanted, copy.wait)

    def pending(i, first_col):
        at = slice(i * nb, i * nb + nb)
        off = first_col - c0
        grid_ref[at, first_col:] = grid_ref[at, first_col:] - three(
            (lcol[0, at, :], lcol[1, at, :]), (rrow[0, :, off:], rrow[1, :, off:]), MM
        )

    def schur(turn):
        if turn == 0:
            upper[0], upper[1] = split2(grid_ref[:c0, c0:])
        elif turn <= rows_dev:
            at = slice(c0 + (turn - 1) * nb, c0 + turn * nb)
            grid_ref[at, c0:] = grid_ref[at, c0:] - three(
                split2(grid_ref[at, :c0]), (upper[0], upper[1]), MM
            )

    def settle(k, here, first_col):
        base = k * nb
        off = first_col - c0
        g = held[...]
        gs = split2(g)
        r = three(split2(three(gs, gs, ((0,), (0,)))), split2(grid_ref[here, first_col:]), MM)
        at = lax.broadcasted_iota(jnp.int32, (rows, nb), 0)
        column = jnp.where((at >= base) & (at < base + nb), 0.0, grid_ref[:rows, here])
        lcol[0], lcol[1] = split2(column)
        rrow[0, :, off:], rrow[1, :, off:] = split2(r)
        grid_ref[here, first_col:] = r

    def step(k, here, filler):
        base = k * nb
        origin[...] = tile[...]
        factor_tile(tile, nb, filler)
        held[...] = jnp.where(ii >= jj, tile[...], 0.0)

        @pl.when(k == my_col)
        def _():
            g = held[...]
            gs = split2(g)
            for a in range(na):
                row = a * rows_dev + my_row

                @pl.when(row == k)
                def _():
                    own = three(split2(origin[...]), gs, ((1,), (1,)))
                    top[a] = jnp.where(ii >= jj, own, 0.0)

                @pl.when(row > k)
                def _():
                    block = grid_ref[here, pl.ds(pl.multiple_of(row * nb, nb), nb)]
                    top[a] = three(gs, split2(block), MM).T

            at = lax.broadcasted_iota(jnp.int32, (rows, nb), 0)
            found = three(split2(grid_ref[:rows, here]), gs, ((1,), (1,)))
            col_ref[:rows, :] = jnp.where(at < base, -found, 0.0)
            col_ref[here, :] = g.T

    here = slice(c0, c0 + nb)
    if phase:
        for wanted, copy in side_copies:
            copy.wait()
        tile[...] = grid_ref[here, here] - three(
            split2(grid_ref[here, :c0]), split2(grid_ref[:c0, here]), MM
        )
        step(phase * rows_dev, here, schur)
    else:
        tile[...] = grid_ref[here, here]

        def arrive(turn):
            if turn == nb // SUB - 1:
                for wanted, copy in side_copies:
                    copy.wait()

        step(0, here, arrive)

    @pl.loop(phase * rows_dev + 1, (phase + 1) * rows_dev)
    def _(k):
        before = pl.ds(pl.multiple_of(k * nb - nb, nb), nb)
        here = pl.ds(pl.multiple_of(k * nb, nb), nb)
        cross = three(split2(held[...]), split2(grid_ref[before, here]), MM)
        tile[...] = grid_ref[here, here] - three(split2(cross), split2(cross), ((0,), (0,)))

        def late(turn):
            if turn == 0:
                settle(k - 1, before, c0)
            turns = nb // SUB - 1
            for i in range(rows // nb):
                if i % turns == turn - 1:
                    pending(i, c0)

        step(k, here, late)

    settle((phase + 1) * rows_dev - 1, slice(rows - nb, rows), lead if last else rows)
    sent = []
    for i in range(rows // nb):
        at = slice(i * nb, i * nb + nb)
        if last:
            pending(i, lead)
            first = col_ref[at, :]
            if not fwd:
                first = jnp.where(my_col < STEPS, first, grid_ref[at, lead : lead + nb])
            solved_buf[0, at, :nb], solved_buf[1, at, :nb] = split2(first)
            solved_buf[0, at, nb:], solved_buf[1, at, nb:] = split2(
                grid_ref[at, lead + (nb if not fwd else 0) :]
            )
            copy = pltpu.make_async_copy(solved_buf.at[:, at, :], solved.at[:, at, :], out_sems.at[i])
        else:
            pending(i, rows)
            copy = pltpu.make_async_copy(grid_ref.at[at, rows:], passed.at[at, :], out_sems.at[i])
        copy.start()
        sent.append(copy)
    for copy in sent:
        copy.wait()


def close_kernel(place, *refs, nb, na, block_rows, block_cols, cols_dev, n_low):
    n_high = cols_dev // n_low
    near = refs[:n_high]
    far0, far, mine, solved, top, out = refs[n_high : n_high + 6]
    raw, old, right, left_h, left_m, made, sems, out_sems = refs[n_high + 6 :]
    my_col = place[1]
    MM = ((1,), (0,))
    always = cols_dev == STEPS
    group = nb * block_cols
    loads = []
    for back_l in range(n_low):
        for back_h in range(n_high):
            n = back_l * n_high + back_h
            across = near[back_h] if back_l == 0 else far0 if back_h == 0 else far.at[back_h - 1]
            col = col_of(my_col, back_h, back_l, cols_dev, n_low)
            copy = pltpu.make_async_copy(across, raw.at[n], sems.at[n])
            guarded(always, col < STEPS, copy.start)
            loads.append((n, col, copy))
    right_copy = pltpu.make_async_copy(solved, right, sems.at[cols_dev])
    right_copy.start()
    old_copy = pltpu.make_async_copy(mine.at[na * group :, :], old, sems.at[cols_dev + 1])
    old_copy.start()

    sent = []

    def send(a):
        at = slice(a * group, a * group + group)
        copy = pltpu.make_async_copy(made.at[at, :], out.at[at, :], out_sems.at[a])
        copy.start()
        sent.append(copy)

    for a in range(na):
        made[a * group : a * group + group, :] = jnp.zeros((group, nb), F32)
        made[pl.ds(a * group, nb, stride=block_cols), :] = top[a]
        send(a)
    for n, col, copy in loads:

        def take():
            copy.wait()
            at = pl.ds(pl.multiple_of(col * nb, nb), nb)
            left_h[:, at], left_m[:, at] = split2(raw[n])

        guarded(always, col < STEPS, take)
    right_copy.wait()
    old_copy.wait()
    is_panel = my_col < STEPS
    below = block_rows - na
    chunk = 3 if below % 3 == 0 else 1
    for first in range(0, below, chunk):
        at = slice(first * nb, (first + chunk) * nb)
        prod = three((left_h[at, :], left_m[at, :]), (right[0], right[1]), MM)
        for i in range(chunk):
            for b in range(block_cols):
                part = prod[i * nb : (i + 1) * nb, b * nb : (b + 1) * nb]
                prior = old[pl.ds((first + i) * group + b, nb, stride=block_cols), :]
                value = prior - part
                if b == 0:
                    value = jnp.where(is_panel, part, value)
                made[pl.ds((first + i + na) * group + b, nb, stride=block_cols), :] = value
            send(first + i + na)
    for copy in sent:
        copy.wait()


def local(matrix):
    rows_dev = lax.axis_size("row")
    cols_dev = lax.axis_size("col")
    my_row = lax.axis_index("row")
    my_col = lax.axis_index("col")
    block_rows, nb, block_cols, _ = matrix.shape
    na = STEPS // rows_dev
    fwd = STEPS // cols_dev
    lead = STEPS * nb
    wide = block_cols * nb
    n_side = block_cols - fwd
    n_low = 2
    n_high = cols_dev // n_low
    place = jnp.stack([my_row, my_col]).astype(jnp.int32)

    def tie(x, *after):
        return lax.optimization_barrier((x,) + after)[0] if after else x

    def step_to(x, axis, size, low, back_high, back_low):
        pairs = []
        for i in range(size):
            high, rest = divmod(i, low)
            pairs.append((i, (high + back_high) % (size // low) * low + (rest + back_low) % low))
        return lax.ppermute(x, axis, pairs)

    def line_of(x, *after):
        x = tie(x, *after)
        return [x] + [step_to(x, "col", cols_dev, n_low, h, 0) for h in range(1, n_high)]

    def across_rows(x, *after):
        x = tie(x, *after)
        return [x] + [step_to(x, "row", rows_dev, 2, h, 0) for h in range(1, rows_dev // 2)]

    def swap_core(x):
        return step_to(x, "row", rows_dev, 2, 0, 1)

    blocks = [matrix[a, :, 0, :] for a in range(na)]
    lines = [line_of(blocks[0])]
    side = across_rows(matrix[:na, :, fwd:, :].transpose(0, 2, 1, 3))
    side = side + [swap_core(x) for x in side]
    strips = []
    for a in range(na):
        if a:
            lines.append(line_of(blocks[a], side[rows_dev // 2]))
        line = jnp.stack(lines[a])
        strips.append(jnp.concatenate([line, step_to(line, "col", cols_dev, n_low, 0, 1)]))
    body = line_of(matrix[na:, :, 0, :].reshape(-1, nb), strips[0])
    body_far = step_to(tie(body[0], strips[0]), "col", cols_dev, n_low, 0, 1)
    phases = []
    for a in range(na):
        near = across_rows(strips[a], *(phases[0][1 : rows_dev // 2] if a else ()))
        phases.append(near + [swap_core(x) for x in near])

    vmem = pl.BlockSpec(memory_space=pltpu.VMEM)
    smem = pl.BlockSpec(memory_space=pltpu.SMEM)
    hbm = pl.BlockSpec(memory_space=pl.ANY)
    params = pltpu.CompilerParams(vmem_limit_bytes=20 << 20)
    carried = []
    for phase, pieces in enumerate(phases):
        last = phase == na - 1
        c0 = phase * rows_dev * nb
        rows = c0 + rows_dev * nb
        width = lead + n_side * nb
        out_shape = [jax.ShapeDtypeStruct((na, nb, nb), F32)]
        if last:
            out_shape = [jax.ShapeDtypeStruct((2, lead, wide), BF16)] + out_shape
        else:
            out_shape = [
                jax.ShapeDtypeStruct((rows, width - rows), F32),
                jax.ShapeDtypeStruct((rows, nb), F32),
            ] + out_shape
        carried = pl.pallas_call(
            functools.partial(
                sweep_kernel,
                phase=phase,
                last=last,
                nb=nb,
                na=na,
                rows_dev=rows_dev,
                cols_dev=cols_dev,
                fwd=fwd,
                n_pieces=len(pieces),
                n_low=n_low,
            ),
            out_shape=out_shape,
            in_specs=[smem] + [hbm] * (2 * len(pieces)) + ([hbm, vmem, vmem] if phase else []),
            out_specs=[hbm] + [vmem] * (len(out_shape) - 1),
            scratch_shapes=(
                [pltpu.VMEM((2, lead, wide), BF16), pltpu.VMEM((lead, nb), F32)] if last else []
            )
            + [
                pltpu.VMEM((rows, width), F32),
                pltpu.VMEM((nb, nb), F32),
                pltpu.VMEM((nb, nb), F32),
                pltpu.VMEM((nb, nb), F32),
                pltpu.VMEM((2, rows, nb), BF16),
                pltpu.VMEM((2, nb, width - c0), BF16),
                pltpu.VMEM((2, max(c0, nb), width - c0), BF16),
                pltpu.SemaphoreType.DMA((len(pieces) * (cols_dev + n_side) + 1,)),
                pltpu.SemaphoreType.DMA((rows // nb,)),
            ],
            compiler_params=params,
            cost_estimate=pl.CostEstimate(flops=3 * 10**9, bytes_accessed=10**7, transcendentals=0),
            name="sweep%d" % phase,
        )(place, *pieces, *side, *carried)
        if phase == 0:
            far = step_to(jnp.stack([tie(x, carried[0], body_far) for x in body[1:]]), "col", cols_dev, n_low, 0, 1)
    solved, top = carried
    out = pl.pallas_call(
        functools.partial(close_kernel, nb=nb, na=na, block_rows=block_rows, block_cols=block_cols, cols_dev=cols_dev, n_low=n_low),
        out_shape=jax.ShapeDtypeStruct((block_rows * nb * block_cols, nb), F32),
        in_specs=[smem] + [hbm] * (n_high + 4) + [vmem],
        out_specs=hbm,
        scratch_shapes=[
            pltpu.VMEM((cols_dev, (block_rows - na) * nb, nb), F32),
            pltpu.VMEM(((block_rows - na) * nb * block_cols, nb), F32),
            pltpu.VMEM((2, lead, wide), BF16),
            pltpu.VMEM(((block_rows - na) * nb, lead), BF16),
            pltpu.VMEM(((block_rows - na) * nb, lead), BF16),
            pltpu.VMEM((block_rows * nb * block_cols, nb), F32),
            pltpu.SemaphoreType.DMA((cols_dev + 2,)),
            pltpu.SemaphoreType.DMA((block_rows,)),
        ],
        compiler_params=params,
        name="close",
    )(place, *body, body_far, far, matrix.reshape(-1, nb), solved, top)
    return out.reshape(matrix.shape)


def solution(mesh):
    placed = (P(None, "row", None, "col"),)
    return jax.shard_map(
        local, mesh=mesh, in_specs=placed, out_specs=P(None, "row", None, "col"), check_vma=False
    )
```

```python
import functools

import jax
import jax.numpy as jnp
from jax import lax
from jax.experimental import pallas as pl
from jax.experimental.pallas import tpu as pltpu
from jax.sharding import PartitionSpec as P

STEPS = 8
PANELS = (64, 32)
SUB = 8
F32 = jnp.float32
BF16 = jnp.bfloat16


def split2(x):
    high = x.astype(BF16)
    return high, (x - high.astype(F32)).astype(BF16)


def split3(x):
    high = x.astype(BF16)
    rest = x - high.astype(F32)
    mid = rest.astype(BF16)
    return high, mid, (rest - mid.astype(F32)).astype(BF16)


def contract(left, right, dims):
    return lax.dot_general(left, right, (dims, ((), ())), preferred_element_type=F32)


def gram(rows_in, rows_wide):
    h, m, l = split3(rows_in)
    hw, mw, lw = split3(rows_wide)
    left = jnp.concatenate([h, h, m, m, h, l], 0)
    right = jnp.concatenate([hw, mw, hw, mw, lw, hw], 0)
    return contract(left, right, ((0,), (0,)))


def three(left, right, dims):
    (lh, lm), (rh, rm) = left, right
    return contract(lh, rh, dims) + (contract(lh, rm, dims) + contract(lm, rh, dims))


def factor_tile(tile, nb, panel, filler):
    lane = lax.broadcasted_iota(jnp.int32, (SUB, nb), 1)
    sub = lax.broadcasted_iota(jnp.int32, (SUB, nb), 0)
    count = panel // SUB
    for first in range(0, nb, panel):
        after = first + panel
        parts = [tile[first + SUB * v : first + SUB * v + SUB, :] for v in range(count)]
        for b in range(count):
            at = first + SUB * b
            inside = (lane >= at) & (lane < at + SUB)
            row = [jnp.broadcast_to(parts[b][i : i + 1, :], (SUB, nb)) for i in range(SUB)]
            entry = {}
            for i in range(SUB):
                for s in range(i + 1):
                    entry[i, s] = jnp.broadcast_to(row[s][:, at + i : at + i + 1], (SUB, nb))
            below = [
                [jnp.broadcast_to(parts[v][:, at + t : at + t + 1], (SUB, nb)) for t in range(SUB)]
                for v in range(b + 1, count)
            ]
            row = [
                jnp.where(inside, jnp.where(lane == at + i, 1.0, 0.0), row[i]) for i in range(SUB)
            ]
            for s in range(SUB):
                scale = lax.rsqrt(entry[s, s])
                row[s] = row[s] * scale
                for column in below:
                    column[s] = column[s] * scale
                for i in range(s + 1, SUB):
                    entry[i, s] = entry[i, s] * scale
                for i in range(s + 1, SUB):
                    for t in range(s + 1, i + 1):
                        entry[i, t] = entry[i, t] - entry[i, s] * entry[t, s]
                for i in range(s + 1, SUB):
                    row[i] = row[i] - entry[i, s] * row[s]
                for column in below:
                    for t in range(s + 1, SUB):
                        column[t] = column[t] - column[s] * entry[t, s]
            made = row[0]
            for s in range(1, SUB):
                made = jnp.where(sub == s, row[s], made)
            for v, column in zip(range(b + 1, count), below):
                terms = [column[s] * row[s] for s in range(SUB)]
                while len(terms) > 1:
                    terms = [terms[n] + terms[n + 1] for n in range(0, len(terms), 2)]
                parts[v] = jnp.where(inside, 0.0, parts[v]) - terms[0]
            parts[b] = jnp.where((lane >= at + SUB) & (lane < after), 0.0, made)
            filler((first + SUB * b) // SUB)
        done = jnp.concatenate(parts, 0)
        tile[first:after, :] = done
        if after < nb:
            kept = lax.broadcasted_iota(jnp.int32, (nb - after, nb), 1)
            kept = (kept < first) | (kept >= after)
            tile[after:, :] = jnp.where(kept, tile[after:, :], 0.0) - gram(done, done)[after:, :]


def col_of(my_col, back_h, back_l, cols_dev, n_low):
    n_high = cols_dev // n_low
    high = lax.rem(my_col // n_low - back_h + n_high, n_high)
    return high * n_low + lax.rem(lax.rem(my_col, n_low) - back_l + n_low, n_low)


def guarded(always, condition, action):
    if always:
        action()
    else:
        pl.when(condition)(action)


def sweep_kernel(*refs, phase, last, nb, na, rows_dev, cols_dev, fwd, n_pieces, n_low):
    place = refs[0]
    pieces = refs[1 : 1 + n_pieces]
    sides = refs[1 + n_pieces : 1 + 2 * n_pieces]
    refs = refs[1 + 2 * n_pieces :]
    if phase:
        old, old_col, old_top = refs[:3]
        refs = refs[3:]
    if last:
        solved, top, solved_buf, col_ref = refs[:4]
        refs = refs[4:]
    else:
        passed, col_ref, top = refs[:3]
        refs = refs[3:]
    grid_ref, tile, held, origin, lcol, rrow, upper, sems, out_sems = refs
    my_row, my_col = place[0], place[1]
    lead = STEPS * nb
    c0 = phase * rows_dev * nb
    rows = c0 + rows_dev * nb
    n_side = sides[0].shape[1]
    ii = lax.broadcasted_iota(jnp.int32, (nb, nb), 0)
    jj = lax.broadcasted_iota(jnp.int32, (nb, nb), 1)
    MM = ((1,), (0,))

    lead_copies = []
    side_copies = []
    n_high = cols_dev // n_low
    for array, side, (back_hi, back_lo) in zip(
        pieces, sides, [(h, l) for l in range(2) for h in range(rows_dev // 2)], strict=True
    ):
        row_hi = lax.rem(my_row // 2 - back_hi + rows_dev // 2, rows_dev // 2)
        row_lo = lax.rem(lax.rem(my_row, 2) + back_lo, 2)
        at = pl.multiple_of(c0 + (row_hi * 2 + row_lo) * nb, nb)
        for i in range(cols_dev):
            col = col_of(my_col, i % n_high, i // n_high, cols_dev, n_low)
            copy = pltpu.make_async_copy(
                array.at[i],
                grid_ref.at[pl.ds(at, nb), pl.ds(pl.multiple_of(col * nb, nb), nb)],
                sems.at[len(lead_copies) + len(side_copies)],
            )
            lead_copies.append((col < STEPS, copy))
        for b in range(n_side):
            copy = pltpu.make_async_copy(
                side.at[phase, b],
                grid_ref.at[pl.ds(at, nb), lead + b * nb : lead + b * nb + nb],
                sems.at[len(lead_copies) + len(side_copies)],
            )
            side_copies.append((True, copy))
    if phase:
        copy = pltpu.make_async_copy(
            old, grid_ref.at[:c0, c0:], sems.at[len(lead_copies) + len(side_copies)]
        )
        lead_copies.append((True, copy))
    always = cols_dev == STEPS
    for wanted, copy in lead_copies + side_copies:
        guarded(always or wanted is True, wanted, copy.start)
    if phase:
        col_ref[:c0, :] = old_col[...]
        col_ref[c0:, :] = jnp.zeros((lead - c0, nb), F32)
        top[...] = old_top[...]
    else:
        col_ref[...] = jnp.zeros(col_ref.shape, F32)
        top[...] = jnp.zeros(top.shape, F32)
    for wanted, copy in lead_copies:
        guarded(always or wanted is True, wanted, copy.wait)

    def pending(i, first_col):
        at = slice(i * nb, i * nb + nb)
        off = first_col - c0
        grid_ref[at, first_col:] = grid_ref[at, first_col:] - three(
            (lcol[0, at, :], lcol[1, at, :]), (rrow[0, :, off:], rrow[1, :, off:]), MM
        )

    def schur(turn):
        if turn == 0:
            upper[0], upper[1] = split2(grid_ref[:c0, c0:])
        elif turn <= rows_dev:
            at = slice(c0 + (turn - 1) * nb, c0 + turn * nb)
            grid_ref[at, c0:] = grid_ref[at, c0:] - three(
                split2(grid_ref[at, :c0]), (upper[0], upper[1]), MM
            )

    def settle(k, here, first_col):
        base = k * nb
        off = first_col - c0
        g = held[...]
        gs = split2(g)
        r = three(split2(three(gs, gs, ((0,), (0,)))), split2(grid_ref[here, first_col:]), MM)
        at = lax.broadcasted_iota(jnp.int32, (rows, nb), 0)
        column = jnp.where((at >= base) & (at < base + nb), 0.0, grid_ref[:rows, here])
        lcol[0], lcol[1] = split2(column)
        rrow[0, :, off:], rrow[1, :, off:] = split2(r)
        grid_ref[here, first_col:] = r

    def step(k, here, filler):
        base = k * nb
        origin[...] = tile[...]
        factor_tile(tile, nb, PANELS[min(phase, 1)], filler)
        held[...] = jnp.where(ii >= jj, tile[...], 0.0)

        @pl.when(k == my_col)
        def _():
            g = held[...]
            gs = split2(g)
            for a in range(na):
                row = a * rows_dev + my_row

                @pl.when(row == k)
                def _():
                    own = three(split2(origin[...]), gs, ((1,), (1,)))
                    top[a] = jnp.where(ii >= jj, own, 0.0)

                @pl.when(row > k)
                def _():
                    block = grid_ref[here, pl.ds(pl.multiple_of(row * nb, nb), nb)]
                    top[a] = three(gs, split2(block), MM).T

            at = lax.broadcasted_iota(jnp.int32, (rows, nb), 0)
            found = three(split2(grid_ref[:rows, here]), gs, ((1,), (1,)))
            col_ref[:rows, :] = jnp.where(at < base, -found, 0.0)
            col_ref[here, :] = g.T

    here = slice(c0, c0 + nb)
    if phase:
        for wanted, copy in side_copies:
            copy.wait()
        tile[...] = grid_ref[here, here] - three(
            split2(grid_ref[here, :c0]), split2(grid_ref[:c0, here]), MM
        )
        step(phase * rows_dev, here, schur)
    else:
        tile[...] = grid_ref[here, here]

        def arrive(turn):
            if turn == nb // SUB - 1:
                for wanted, copy in side_copies:
                    copy.wait()

        step(0, here, arrive)

    @pl.loop(phase * rows_dev + 1, (phase + 1) * rows_dev)
    def _(k):
        before = pl.ds(pl.multiple_of(k * nb - nb, nb), nb)
        here = pl.ds(pl.multiple_of(k * nb, nb), nb)
        cross = three(split2(held[...]), split2(grid_ref[before, here]), MM)
        tile[...] = grid_ref[here, here] - three(split2(cross), split2(cross), ((0,), (0,)))

        def late(turn):
            if turn == 0:
                settle(k - 1, before, c0)
            turns = nb // SUB - 1
            for i in range(rows // nb):
                if i % turns == turn - 1:
                    pending(i, c0)

        step(k, here, late)

    settle((phase + 1) * rows_dev - 1, slice(rows - nb, rows), lead if last else rows)
    sent = []
    for i in range(rows // nb):
        at = slice(i * nb, i * nb + nb)
        if last:
            pending(i, lead)
            first = col_ref[at, :]
            if not fwd:
                first = jnp.where(my_col < STEPS, first, grid_ref[at, lead : lead + nb])
            solved_buf[0, at, :nb], solved_buf[1, at, :nb] = split2(first)
            solved_buf[0, at, nb:], solved_buf[1, at, nb:] = split2(
                grid_ref[at, lead + (nb if not fwd else 0) :]
            )
            copy = pltpu.make_async_copy(solved_buf.at[:, at, :], solved.at[:, at, :], out_sems.at[i])
        else:
            pending(i, rows)
            copy = pltpu.make_async_copy(grid_ref.at[at, rows:], passed.at[at, :], out_sems.at[i])
        copy.start()
        sent.append(copy)
    for copy in sent:
        copy.wait()


def close_kernel(place, *refs, nb, na, block_rows, block_cols, cols_dev, n_low):
    n_high = cols_dev // n_low
    near = refs[:n_high]
    far0, far, mine, solved, top, out = refs[n_high : n_high + 6]
    raw, old, right, left_h, left_m, made, sems, out_sems = refs[n_high + 6 :]
    my_col = place[1]
    MM = ((1,), (0,))
    always = cols_dev == STEPS
    group = nb * block_cols
    loads = []
    for back_l in range(n_low):
        for back_h in range(n_high):
            n = back_l * n_high + back_h
            across = near[back_h] if back_l == 0 else far0 if back_h == 0 else far.at[back_h - 1]
            col = col_of(my_col, back_h, back_l, cols_dev, n_low)
            copy = pltpu.make_async_copy(across, raw.at[n], sems.at[n])
            guarded(always, col < STEPS, copy.start)
            loads.append((n, col, copy))
    right_copy = pltpu.make_async_copy(solved, right, sems.at[cols_dev])
    right_copy.start()
    old_copy = pltpu.make_async_copy(mine.at[na * group :, :], old, sems.at[cols_dev + 1])
    old_copy.start()

    sent = []

    def send(a):
        at = slice(a * group, a * group + group)
        copy = pltpu.make_async_copy(made.at[at, :], out.at[at, :], out_sems.at[a])
        copy.start()
        sent.append(copy)

    for a in range(na):
        made[a * group : a * group + group, :] = jnp.zeros((group, nb), F32)
        made[pl.ds(a * group, nb, stride=block_cols), :] = top[a]
        send(a)
    for n, col, copy in loads:

        def take():
            copy.wait()
            at = pl.ds(pl.multiple_of(col * nb, nb), nb)
            left_h[:, at], left_m[:, at] = split2(raw[n])

        guarded(always, col < STEPS, take)
    right_copy.wait()
    old_copy.wait()
    is_panel = my_col < STEPS
    below = block_rows - na
    chunk = 3 if below % 3 == 0 else 1
    for first in range(0, below, chunk):
        at = slice(first * nb, (first + chunk) * nb)
        prod = three((left_h[at, :], left_m[at, :]), (right[0], right[1]), MM)
        for i in range(chunk):
            for b in range(block_cols):
                part = prod[i * nb : (i + 1) * nb, b * nb : (b + 1) * nb]
                prior = old[pl.ds((first + i) * group + b, nb, stride=block_cols), :]
                value = prior - part
                if b == 0:
                    value = jnp.where(is_panel, part, value)
                made[pl.ds((first + i + na) * group + b, nb, stride=block_cols), :] = value
            send(first + i + na)
    for copy in sent:
        copy.wait()


def local(matrix):
    rows_dev = lax.axis_size("row")
    cols_dev = lax.axis_size("col")
    my_row = lax.axis_index("row")
    my_col = lax.axis_index("col")
    block_rows, nb, block_cols, _ = matrix.shape
    na = STEPS // rows_dev
    fwd = STEPS // cols_dev
    lead = STEPS * nb
    wide = block_cols * nb
    n_side = block_cols - fwd
    n_low = 2
    n_high = cols_dev // n_low
    place = jnp.stack([my_row, my_col]).astype(jnp.int32)

    def tie(x, *after):
        return lax.optimization_barrier((x,) + after)[0] if after else x

    def step_to(x, axis, size, low, back_high, back_low):
        pairs = []
        for i in range(size):
            high, rest = divmod(i, low)
            pairs.append((i, (high + back_high) % (size // low) * low + (rest + back_low) % low))
        return lax.ppermute(x, axis, pairs)

    def line_of(x, *after):
        x = tie(x, *after)
        return [x] + [step_to(x, "col", cols_dev, n_low, h, 0) for h in range(1, n_high)]

    def across_rows(x, *after):
        x = tie(x, *after)
        return [x] + [step_to(x, "row", rows_dev, 2, h, 0) for h in range(1, rows_dev // 2)]

    def swap_core(x):
        return step_to(x, "row", rows_dev, 2, 0, 1)

    blocks = [matrix[a, :, 0, :] for a in range(na)]
    lines = [line_of(blocks[0])]
    side = across_rows(matrix[:na, :, fwd:, :].transpose(0, 2, 1, 3))
    side = side + [swap_core(x) for x in side]
    strips = []
    for a in range(na):
        if a:
            lines.append(line_of(blocks[a], side[rows_dev // 2]))
        line = jnp.stack(lines[a])
        strips.append(jnp.concatenate([line, step_to(line, "col", cols_dev, n_low, 0, 1)]))
    body = line_of(matrix[na:, :, 0, :].reshape(-1, nb), strips[0])
    body_far = step_to(tie(body[0], strips[0]), "col", cols_dev, n_low, 0, 1)
    phases = []
    for a in range(na):
        near = across_rows(strips[a], *(phases[0][1 : rows_dev // 2] if a else ()))
        phases.append(near + [swap_core(x) for x in near])

    vmem = pl.BlockSpec(memory_space=pltpu.VMEM)
    smem = pl.BlockSpec(memory_space=pltpu.SMEM)
    hbm = pl.BlockSpec(memory_space=pl.ANY)
    params = pltpu.CompilerParams(vmem_limit_bytes=20 << 20)
    carried = []
    for phase, pieces in enumerate(phases):
        last = phase == na - 1
        c0 = phase * rows_dev * nb
        rows = c0 + rows_dev * nb
        width = lead + n_side * nb
        out_shape = [jax.ShapeDtypeStruct((na, nb, nb), F32)]
        if last:
            out_shape = [jax.ShapeDtypeStruct((2, lead, wide), BF16)] + out_shape
        else:
            out_shape = [
                jax.ShapeDtypeStruct((rows, width - rows), F32),
                jax.ShapeDtypeStruct((rows, nb), F32),
            ] + out_shape
        carried = pl.pallas_call(
            functools.partial(
                sweep_kernel,
                phase=phase,
                last=last,
                nb=nb,
                na=na,
                rows_dev=rows_dev,
                cols_dev=cols_dev,
                fwd=fwd,
                n_pieces=len(pieces),
                n_low=n_low,
            ),
            out_shape=out_shape,
            in_specs=[smem] + [hbm] * (2 * len(pieces)) + ([hbm, vmem, vmem] if phase else []),
            out_specs=[hbm] + [vmem] * (len(out_shape) - 1),
            scratch_shapes=(
                [pltpu.VMEM((2, lead, wide), BF16), pltpu.VMEM((lead, nb), F32)] if last else []
            )
            + [
                pltpu.VMEM((rows, width), F32),
                pltpu.VMEM((nb, nb), F32),
                pltpu.VMEM((nb, nb), F32),
                pltpu.VMEM((nb, nb), F32),
                pltpu.VMEM((2, rows, nb), BF16),
                pltpu.VMEM((2, nb, width - c0), BF16),
                pltpu.VMEM((2, max(c0, nb), width - c0), BF16),
                pltpu.SemaphoreType.DMA((len(pieces) * (cols_dev + n_side) + 1,)),
                pltpu.SemaphoreType.DMA((rows // nb,)),
            ],
            compiler_params=params,
            cost_estimate=pl.CostEstimate(flops=3 * 10**9, bytes_accessed=10**7, transcendentals=0),
            name="sweep%d" % phase,
        )(place, *pieces, *side, *carried)
        if phase == 0:
            far = step_to(jnp.stack([tie(x, carried[0], body_far) for x in body[1:]]), "col", cols_dev, n_low, 0, 1)
    solved, top = carried
    out = pl.pallas_call(
        functools.partial(close_kernel, nb=nb, na=na, block_rows=block_rows, block_cols=block_cols, cols_dev=cols_dev, n_low=n_low),
        out_shape=jax.ShapeDtypeStruct((block_rows * nb * block_cols, nb), F32),
        in_specs=[smem] + [hbm] * (n_high + 4) + [vmem],
        out_specs=hbm,
        scratch_shapes=[
            pltpu.VMEM((cols_dev, (block_rows - na) * nb, nb), F32),
            pltpu.VMEM(((block_rows - na) * nb * block_cols, nb), F32),
            pltpu.VMEM((2, lead, wide), BF16),
            pltpu.VMEM(((block_rows - na) * nb, lead), BF16),
            pltpu.VMEM(((block_rows - na) * nb, lead), BF16),
            pltpu.VMEM((block_rows * nb * block_cols, nb), F32),
            pltpu.SemaphoreType.DMA((cols_dev + 2,)),
            pltpu.SemaphoreType.DMA((block_rows,)),
        ],
        compiler_params=params,
        name="close",
    )(place, *body, body_far, far, matrix.reshape(-1, nb), solved, top)
    return out.reshape(matrix.shape)


def solution(mesh):
    placed = (P(None, "row", None, "col"),)
    return jax.shard_map(
        local, mesh=mesh, in_specs=placed, out_specs=P(None, "row", None, "col"), check_vma=False
    )
```
